32 devices in a mesh: kv: 2 (over x), seq: 16 (over z, y, core).
Axes of the slice: x: 2, y: 2, z: 4, core: 2. Of those that a mesh axis runs over, the one named last changes fastest.
Arguments:
- hidden: bfloat16 [1024, 2048], P('seq', 'kv'), may hold values from -1.5 to 1.5
- in_gain: float32 [2048], replicated, may hold values from 0.5 to 1.5
- w_query: bfloat16 [2048, 2048], P(None, 'kv'), may hold values from -0.125 to 0.125
- key_projection_weight: bfloat16 [2048, 1024], P(None, 'kv'), may hold values from -0.125 to 0.125
- value_projection_weight: bfloat16 [2048, 1024], P(None, 'kv'), may hold values from -0.125 to 0.125
- w_gate: bfloat16 [2048, 16], P(None, 'kv'), may hold values from -0.125 to 0.125
- w_out: bfloat16 [2048, 2048], P('kv'), may hold values from -0.125 to 0.125
- q_gain: float32 [128], replicated, may hold values from 0.1 to 1.9
- k_gain: float32 [128], replicated, may hold values from 0.1 to 1.9
- cache_keys: bfloat16 [32768, 8, 128], P('seq', 'kv'), may hold values from -160 to 160
- pooled_cache_values: bfloat16 [32768, 8, 128], P('seq', 'kv'), may hold values from -6 to 6
- prefix_len: int32 [4], replicated, may hold values from 1024 to 8192, as said below
- own_len: int32 [32], replicated, may hold values from 256 to 2048, as said below
- request_group: int32 [32], replicated, may hold values from 0 to 3, as said below
- parents: int32 [32, 32], P('seq'), may hold values from 0 to 30, as said below
- accepted_leaf: int32 [32], P('seq'), may hold values from 0 to 31
Outputs:
- layer_out: bfloat16 [1024, 2048], P('seq', 'kv')
- accepted_keys: bfloat16 [32, 32, 1024], P('seq', None, 'kv')
- accepted_values: bfloat16 [32, 32, 1024], P('seq', None, 'kv')
The draws below stay inside these ranges and needn't reach their ends.
Inputs may be any that keep to these rules, and one draw needn't show every extreme that they name: parents[r, 0] is 0 and node 0 is the root; for i >= 1, parents[r, i] < i. `prefix_len`: the lengths sum to 32768 // 2; one is exactly 8192 and one exactly 1024. `own_len`: the lengths sum to 32768 // 2; one is exactly 2048 and one exactly 256. `request_group`: every group holds exactly 8 requests.
All inputs are finite; a program needn't handle non-finite values.
Results may differ from the reference program's by a relative error of at most 0.017.
The reference program's roundings to bfloat16 on the way count: a program that leaves them out, or rounds other values in their place, can miss the bound.
Values may be sent and summed in bfloat16 or wider, within the bound.
A program may use at most 128 MiB of HBM per device.

```python
import math
import jax
import jax.numpy as jnp
from jax import lax

MODEL_WIDTH = 2048
HQ = 16
KEY_VALUE_HEADS = 8
HEAD_SIZE = 128
TREE = 32
R = 32
TOKENS = 1024
CACHE_SLOTS = 32768
GROUPS = 4
PRE_MOST = 8192
PRE_LEAST = 1024
OWN_MOST = 2048
OWN_LEAST = 256


def draw_parents(key, part):
    nodes = jnp.arange(TREE, dtype=jnp.int32)
    upper = jnp.maximum(nodes, 1)
    picked = jax.random.randint(key, (R, TREE), 0, upper[None, :])
    picked = jnp.where(nodes[None, :] > 0, picked, 0).astype(jnp.int32)
    chosen = jax.random.randint(jax.random.fold_in(key, 3), (), 0, R)
    rows = jnp.arange(R, dtype=jnp.int32)
    deepest = (rows[:, None] == chosen) & (nodes[None, :] == TREE - 1)
    return jnp.where(deepest, TREE - 2, picked).astype(jnp.int32)


def draw_cache_keys(key, part):
    base_offset = jnp.clip(jax.random.normal(key, (CACHE_SLOTS, KEY_VALUE_HEADS, HEAD_SIZE), jnp.float32), -4.0, 4.0)
    return (base_offset * 2.5).astype(jnp.bfloat16)


def fill_lengths(key, count, total, most, floor_limit):
    order = jax.random.permutation(jax.random.fold_in(key, 11), count).astype(jnp.int32)
    places = jnp.arange(count, dtype=jnp.int32)
    sorted_index = jnp.zeros((count,), jnp.int32).at[order].set(places)
    weights = jax.random.randint(jax.random.fold_in(key, 12), (count,), 500, 1000).astype(jnp.int32)
    unfilled_entries = sorted_index >= 2
    weights = jnp.where(unfilled_entries, weights, 0)
    extra = total - most - floor_limit * (count - 1)
    common_prefix_part = weights * extra // jnp.sum(weights)
    leftover_number = extra - jnp.sum(common_prefix_part)
    extra_symbol = (unfilled_entries & (sorted_index < 2 + leftover_number)).astype(jnp.int32)
    query_spans = floor_limit + common_prefix_part + extra_symbol
    return jnp.where(sorted_index == 0, most, query_spans).astype(jnp.int32)


def draw_prefix_len(key, part):
    return fill_lengths(key, GROUPS, CACHE_SLOTS // 2, PRE_MOST, PRE_LEAST)


def draw_own_len(key, part):
    return fill_lengths(key, R, CACHE_SLOTS // 2, OWN_MOST, OWN_LEAST)


def draw_request_group(key, part):
    order = jax.random.permutation(jax.random.fold_in(key, 21), R).astype(jnp.int32)
    return (order // 8).astype(jnp.int32)


def plant(array, key, smallest, largest):
    spot = [jax.random.randint(jax.random.fold_in(key, axis), (), 0, length) for axis, length in enumerate(array.shape)]
    longest = array.shape.index(max(array.shape))
    next_to = spot[:longest] + [(spot[longest] + 1) % array.shape[longest]] + spot[longest + 1:]
    return array.at[tuple(spot)].set(smallest).at[tuple(next_to)].set(largest)


def block_levels(stream_key, shape, shards, smallest, largest):
    def one(dim, parts):
        steps = jax.random.uniform(jax.random.fold_in(jax.random.fold_in(stream_key, 6), dim), (parts,), jnp.float32, smallest / len(shards), largest / len(shards))
        return jnp.repeat(jnp.exp(steps), shape[dim] // parts).reshape((-1,) + (1,) * (len(shape) - dim - 1))

    factor_of = one(*shards[0])
    for cut in shards[1:]:
        factor_of = factor_of * one(*cut)
    return factor_of


def scatter_about(key, shape, spread, most, split=(), held_as=jnp.bfloat16):
    array = spread * jax.random.normal(key, shape, jnp.float32)
    if split:
        array = array * block_levels(key, shape, split, -0.22, 0.18)
    return jnp.clip(array, -most, most).astype(held_as)


def setup_inputs(seed: int = 0) -> dict:
    keys = jax.random.split(jax.random.key(seed), 17)
    return {
        "hidden": scatter_about(keys[0], (TOKENS, MODEL_WIDTH), 0.25, 1.5, ((0, 16), (1, 2))),
        "in_gain": jnp.clip(1.0 + 0.1 * jax.random.normal(keys[1], (MODEL_WIDTH,), jnp.float32), 0.5, 1.5),
        "w_query": scatter_about(keys[2], (MODEL_WIDTH, HQ * HEAD_SIZE), MODEL_WIDTH ** -0.5, 0.125, ((1, 2),)),
        "key_projection_weight": scatter_about(keys[3], (MODEL_WIDTH, KEY_VALUE_HEADS * HEAD_SIZE), MODEL_WIDTH ** -0.5, 0.125, ((1, 2),)),
        "value_projection_weight": scatter_about(keys[4], (MODEL_WIDTH, KEY_VALUE_HEADS * HEAD_SIZE), MODEL_WIDTH ** -0.5, 0.125, ((1, 2),)),
        "w_gate": scatter_about(keys[5], (MODEL_WIDTH, HQ), MODEL_WIDTH ** -0.5, 0.125, ((1, 2),)),
        "w_out": scatter_about(keys[6], (HQ * HEAD_SIZE, MODEL_WIDTH), (HQ * HEAD_SIZE) ** -0.5, 0.125, ((0, 2),)),
        "q_gain": jnp.clip(1.0 + 0.18 * jax.random.normal(keys[7], (HEAD_SIZE,), jnp.float32), 0.1, 1.9),
        "k_gain": jnp.clip(1.0 + 0.18 * jax.random.normal(keys[8], (HEAD_SIZE,), jnp.float32), 0.1, 1.9),
        "cache_keys": draw_cache_keys(jax.random.fold_in(keys[16], 71), 0),
        "pooled_cache_values": scatter_about(keys[10], (CACHE_SLOTS, KEY_VALUE_HEADS, HEAD_SIZE), 1.0, 6.0, ((0, 16), (1, 2))),
        "prefix_len": draw_prefix_len(jax.random.fold_in(keys[16], 71), 0),
        "own_len": draw_own_len(jax.random.fold_in(keys[16], 71), 0),
        "request_group": draw_request_group(jax.random.fold_in(keys[16], 71), 0),
        "parents": draw_parents(jax.random.fold_in(keys[16], 71), 0),
        "accepted_leaf": plant(jax.random.randint(keys[15], (R,), 0, TREE), jax.random.fold_in(keys[15], 1), 0, TREE - 1).astype(jnp.int32),
    }


EPSILON = 1e-06
ROPE_BASE = 1000000.0
NEGATIVE = -1e+30

def rms_scale(values, scales):
    mean_square = lax.optimization_barrier(jnp.mean(values * values, axis=-1, keepdims=True))
    return values * lax.rsqrt(mean_square + EPSILON) * scales

def rotate_pairs(values, positions):
    half_width = values.shape[-1] // 2
    freqs = jnp.exp(jnp.arange(half_width, dtype=jnp.float32) * (-2.0 * math.log(ROPE_BASE) / values.shape[-1]))
    angles = positions[:, None] * freqs[None, :]
    cosine = jnp.concatenate([jnp.cos(angles), jnp.cos(angles)], axis=-1)[:, None, :]
    sine = jnp.concatenate([jnp.sin(angles), jnp.sin(angles)], axis=-1)[:, None, :]
    turned = jnp.concatenate([-values[..., half_width:], values[..., :half_width]], axis=-1)
    return values * cosine + turned * sine

def tree_paths(parents):
    width = parents.shape[-1]
    nodes = jnp.arange(width, dtype=jnp.int32)
    linked = (parents[:, :, None] == nodes[None, None, :]).astype(jnp.float32)
    identity_mat = jnp.eye(width, dtype=jnp.float32)
    reach = jnp.minimum(identity_mat[None] + linked * (1.0 - identity_mat[None]), 1.0)
    for squaring in range(max(1, (width - 1).bit_length())):
        reach = jnp.minimum(jnp.einsum('mij,mjk->mik', reach, reach, precision=lax.Precision.HIGHEST), 1.0)
    depth_f = lax.optimization_barrier(jnp.sum(reach, axis=-1)) - 1.0
    return (reach, depth_f)

def accepted_rows(reach, depth_f, leaves, tree_rows):
    width = reach.shape[-1]
    nodes = jnp.arange(width, dtype=jnp.int32)
    leaf_pick = (leaves[:, None] == nodes[None, :]).astype(jnp.float32)
    on_path = jnp.einsum('mi,mij->mj', leaf_pick, reach, precision=lax.Precision.HIGHEST)
    levels = (depth_f[:, None, :] == nodes.astype(jnp.float32)[None, :, None]).astype(jnp.float32)
    select = levels * on_path[:, None, :]
    return jnp.einsum('mdj,mjc->mdc', select, tree_rows.astype(jnp.float32), precision=lax.Precision.HIGHEST).astype(jnp.bfloat16)

def reference(hidden, in_gain, w_query, key_projection_weight, value_projection_weight, w_gate, w_out, q_gain, k_gain, cache_keys, pooled_cache_values, prefix_len, own_len, request_group, parents, accepted_leaf):
    requests = own_len.shape[0]
    tree = parents.shape[1]
    heads = w_gate.shape[1]
    head_width = q_gain.shape[0]
    kv_heads = key_projection_weight.shape[1] // head_width
    per_kv = heads // kv_heads
    groups = prefix_len.shape[0]
    score_scale = 1.0 / math.sqrt(head_width)
    normed = rms_scale(hidden.astype(jnp.float32), in_gain).astype(jnp.bfloat16)
    reach, depth_f = tree_paths(parents)
    context = prefix_len[request_group] + own_len
    positions = (context[:, None].astype(jnp.float32) + depth_f).reshape(-1)
    query = jnp.dot(normed, w_query, preferred_element_type=jnp.float32).reshape(-1, heads, head_width)
    query = rotate_pairs(rms_scale(query, q_gain), positions).astype(jnp.bfloat16)
    key_new = jnp.dot(normed, key_projection_weight, preferred_element_type=jnp.float32).reshape(-1, kv_heads, head_width)
    key_new = rotate_pairs(rms_scale(key_new, k_gain), positions).astype(jnp.bfloat16)
    value_new = jnp.dot(normed, value_projection_weight, preferred_element_type=jnp.float32).astype(jnp.bfloat16).reshape(-1, kv_heads, head_width)
    gate_logit = jnp.dot(normed, w_gate, preferred_element_type=jnp.float32)
    lengths_all = jnp.concatenate([prefix_len, own_len]).astype(jnp.int32)
    starts = (jnp.cumsum(lengths_all) - lengths_all).astype(jnp.int32)
    span = max(PRE_MOST, OWN_MOST)
    padding = jnp.zeros((span, kv_heads, head_width), cache_keys.dtype)
    keys_pool = jnp.concatenate([cache_keys, padding], axis=0)
    values_pool = jnp.concatenate([pooled_cache_values, padding], axis=0)
    pre_start = starts[request_group].astype(jnp.int32)
    pre_count = prefix_len[request_group].astype(jnp.int32)
    own_start = starts[groups:].astype(jnp.int32)

    def one_request(inputs):
        q_rows, k_rows, v_rows, reach_rows, first_pre, count_pre, first_own, count_own = inputs
        zero_index = jnp.zeros((), jnp.int32)
        k_pre = lax.dynamic_slice(keys_pool, (first_pre, zero_index, zero_index), (PRE_MOST, kv_heads, head_width))
        v_pre = lax.dynamic_slice(values_pool, (first_pre, zero_index, zero_index), (PRE_MOST, kv_heads, head_width))
        k_own = lax.dynamic_slice(keys_pool, (first_own, zero_index, zero_index), (OWN_MOST, kv_heads, head_width))
        v_own = lax.dynamic_slice(values_pool, (first_own, zero_index, zero_index), (OWN_MOST, kv_heads, head_width))
        keys_all = jnp.concatenate([k_pre, k_own, k_rows], axis=0).astype(jnp.float32)
        values_all = jnp.concatenate([v_pre, v_own, v_rows], axis=0).astype(jnp.float32)
        pre_mask = jnp.arange(PRE_MOST, dtype=jnp.int32) < count_pre
        own_mask = jnp.arange(OWN_MOST, dtype=jnp.int32) < count_own
        visible = jnp.concatenate([jnp.broadcast_to(pre_mask[None, :], (tree, PRE_MOST)), jnp.broadcast_to(own_mask[None, :], (tree, OWN_MOST)), reach_rows > 0.5], axis=1)
        q_grouped = q_rows.reshape(tree, kv_heads, per_kv, head_width).astype(jnp.float32)
        scores = jnp.einsum('tkgd,lkd->kgtl', q_grouped, keys_all) * score_scale
        scores = jnp.where(visible[None, None], scores, NEGATIVE)
        row_max = lax.optimization_barrier(jnp.max(scores, axis=-1, keepdims=True))
        weights = jnp.where(visible[None, None], jnp.exp(scores - row_max), 0.0)
        weight_sum = lax.optimization_barrier(jnp.sum(weights, axis=-1))
        rounded = weights.astype(jnp.bfloat16).astype(jnp.float32)
        summed = jnp.einsum('kgtl,lkd->tkgd', rounded, values_all)
        return summed / jnp.transpose(weight_sum, (2, 0, 1))[..., None]
    mixed = lax.map(one_request, (query.reshape(requests, tree, heads, head_width), key_new.reshape(requests, tree, kv_heads, head_width), value_new.reshape(requests, tree, kv_heads, head_width), reach, pre_start, pre_count, own_start, own_len.astype(jnp.int32)))
    mixed = mixed.reshape(-1, heads, head_width) * jax.nn.sigmoid(gate_logit)[:, :, None]
    attended = mixed.astype(jnp.bfloat16).reshape(-1, heads * head_width)
    layer_out = (jnp.dot(attended, w_out, preferred_element_type=jnp.float32) + hidden.astype(jnp.float32)).astype(jnp.bfloat16)
    tree_rows = jnp.concatenate([key_new.reshape(requests, tree, kv_heads * head_width), value_new.reshape(requests, tree, kv_heads * head_width)], axis=-1)
    picked = accepted_rows(reach, depth_f, accepted_leaf, tree_rows)
    accepted_keys = picked[:, :, :kv_heads * head_width]
    accepted_values = picked[:, :, kv_heads * head_width:]
    return (layer_out, accepted_keys, accepted_values)
```

```python
import functools
import math

import jax
import jax.numpy as jnp
from jax import lax
from jax.experimental import pallas as pl
from jax.experimental.pallas import tpu as pltpu
from jax.sharding import PartitionSpec as P

EPSILON = 1e-06
ROPE_BASE = 1000000.0
NEGATIVE = -1e30


def rms_scale(values, scales):
    mean_square = jnp.mean(values * values, axis=-1, keepdims=True)
    return values * lax.rsqrt(mean_square + EPSILON) * scales


def rotate_pairs(values, positions):
    half_width = values.shape[-1] // 2
    freqs = jnp.exp(
        jnp.arange(half_width, dtype=jnp.float32) * (-2.0 * math.log(ROPE_BASE) / values.shape[-1])
    )
    angles = positions[:, None] * freqs[None, :]
    cosine = jnp.concatenate([jnp.cos(angles), jnp.cos(angles)], axis=-1)[:, None, :]
    sine = jnp.concatenate([jnp.sin(angles), jnp.sin(angles)], axis=-1)[:, None, :]
    turned = jnp.concatenate([-values[..., half_width:], values[..., :half_width]], axis=-1)
    return values * cosine + turned * sine


def tree_paths(parents):
    width = parents.shape[-1]
    nodes = jnp.arange(width, dtype=jnp.int32)
    linked = (parents[:, :, None] == nodes[None, None, :]).astype(jnp.float32)
    identity_mat = jnp.eye(width, dtype=jnp.float32)
    reach = jnp.minimum(identity_mat[None] + linked * (1.0 - identity_mat[None]), 1.0)
    for squaring in range(max(1, (width - 1).bit_length())):
        reach = jnp.minimum(
            jnp.einsum("mij,mjk->mik", reach, reach, precision=lax.Precision.HIGHEST), 1.0
        )
    depth_f = jnp.sum(reach, axis=-1) - 1.0
    return (reach, depth_f)


def accepted_rows(reach, depth_f, leaves, tree_rows):
    width = reach.shape[-1]
    nodes = jnp.arange(width, dtype=jnp.int32)
    leaf_pick = (leaves[:, None] == nodes[None, :]).astype(jnp.float32)
    on_path = jnp.einsum("mi,mij->mj", leaf_pick, reach, precision=lax.Precision.HIGHEST)
    levels = (depth_f[:, None, :] == nodes.astype(jnp.float32)[None, :, None]).astype(jnp.float32)
    select = levels * on_path[:, None, :]
    return jnp.einsum(
        "mdj,mjc->mdc", select, tree_rows.astype(jnp.float32), precision=lax.Precision.HIGHEST
    ).astype(jnp.bfloat16)


def lowest(distance):
    return distance & -distance


def flip(index, distance):
    out = index
    bit = 1
    while bit <= distance:
        if distance & bit:
            out = out + bit * (1 - 2 * ((index // bit) % 2))
        bit *= 2
    return out


def one_bits(count):
    bits = []
    bit = 1
    while bit < count:
        bits.append(bit)
        bit *= 2
    return bits


def greet(me, count):
    barrier = pltpu.get_barrier_semaphore()
    bits = one_bits(count)
    for bit in bits:
        pl.semaphore_signal(barrier, inc=1, device_id={"seq": flip(me, bit)})
    pl.semaphore_wait(barrier, len(bits))


def gather_kernel(count, mine_ref, all_ref, send_sem, recv_sem):
    me = lax.axis_index("seq")
    all_ref[me] = mine_ref[...]
    greet(me, count)

    def message(distance, owner):
        return pltpu.make_async_remote_copy(
            src_ref=all_ref.at[owner],
            dst_ref=all_ref.at[owner],
            send_sem=send_sem.at[distance],
            recv_sem=recv_sem.at[distance],
            device_id={"seq": flip(me, lowest(distance))},
        )

    sent = []
    order = sorted(range(1, count), key=lambda d: (-lowest(d), d))
    for held in [0] + order:
        owner = flip(me, held)
        if held:
            message(held, owner).wait_recv()
        top = lowest(held) if held else count
        for bit in reversed(one_bits(top)):
            copy = message(held | bit, owner)
            copy.start()
            sent.append(copy)
    for copy in sent:
        copy.wait_send()


def gather_rows(mine, count):
    return pl.pallas_call(
        functools.partial(gather_kernel, count),
        out_shape=jax.ShapeDtypeStruct((count,) + mine.shape, mine.dtype),
        in_specs=[pl.BlockSpec(memory_space=pltpu.VMEM)],
        out_specs=pl.BlockSpec(memory_space=pltpu.VMEM),
        scratch_shapes=[pltpu.SemaphoreType.DMA((count,)), pltpu.SemaphoreType.DMA((count,))],
        compiler_params=pltpu.CompilerParams(
            collective_id=0, has_side_effects=True, vmem_limit_bytes=48 * 2**20
        ),
        name="gather_queries",
    )(mine)


def merge_kernel(
    count, part_ref, lse_ref, out_ref, out_lse_ref, got, got_lse, held, held_lse, send_sem, recv_sem
):
    me = lax.axis_index("seq")
    heads = part_ref.shape[2] // 128
    greet(me, count)

    def messages(distance):
        owner = flip(me, distance)
        if distance % 2:
            sources = (part_ref.at[owner], lse_ref.at[owner])
        else:
            sources = (held.at[distance // 2], held_lse.at[distance // 2])
        return [
            pltpu.make_async_remote_copy(
                src_ref=source,
                dst_ref=target.at[distance],
                send_sem=send_sem.at[which, distance],
                recv_sem=recv_sem.at[which, distance],
                device_id={"seq": flip(me, lowest(distance))},
            )
            for which, (source, target) in enumerate(zip(sources, (got, got_lse)))
        ]

    sent = []

    def send(distance):
        for copy in messages(distance):
            copy.start()
            sent.append(copy)

    for distance in sorted(range(1, count, 2), reverse=True):
        send(distance)
    evens = sorted(range(2, count, 2), key=lambda d: (lowest(d), -d))
    for distance in evens + [0]:
        owner = flip(me, distance)
        incoming = [distance | bit for bit in one_bits(lowest(distance) if distance else count)]
        for message in incoming:
            for copy in messages(message):
                copy.wait_recv()
        levels = [lse_ref[owner]] + [got_lse[message] for message in incoming]
        top = functools.reduce(jnp.maximum, levels)
        shares = [jnp.exp(level - top) for level in levels]
        total = functools.reduce(jnp.add, shares)
        inverse = 1.0 / total
        shares = [share * inverse for share in shares]
        new_lse = top + jnp.log(total)
        if distance:
            held_lse[distance // 2] = new_lse
        else:
            out_lse_ref[...] = new_lse
        for head in range(heads):
            cols = slice(head * 128, (head + 1) * 128)
            pieces = [part_ref[owner, :, cols]] + [got[message, :, cols] for message in incoming]
            mixed = functools.reduce(
                jnp.add,
                [
                    piece.astype(jnp.float32) * share[:, head : head + 1]
                    for piece, share in zip(pieces, shares)
                ],
            )
            if distance:
                held[distance // 2, :, cols] = mixed.astype(held.dtype)
            else:
                out_ref[:, cols] = mixed
        if distance:
            send(distance)
    for copy in sent:
        copy.wait_send()


def merge_parts(parts, lse, count):
    rows, width = parts.shape[1:]
    lanes = lse.shape[2]
    half = max(1, count // 2)
    vmem = pl.BlockSpec(memory_space=pltpu.VMEM)
    return pl.pallas_call(
        functools.partial(merge_kernel, count),
        out_shape=(
            jax.ShapeDtypeStruct((rows, width), jnp.float32),
            jax.ShapeDtypeStruct((rows, lanes), jnp.float32),
        ),
        in_specs=[vmem, vmem],
        out_specs=(vmem, vmem),
        scratch_shapes=[
            pltpu.VMEM((count, rows, width), parts.dtype),
            pltpu.VMEM((count, rows, lanes), jnp.float32),
            pltpu.VMEM((half, rows, width), parts.dtype),
            pltpu.VMEM((half, rows, lanes), jnp.float32),
            pltpu.SemaphoreType.DMA((2, count)),
            pltpu.SemaphoreType.DMA((2, count)),
        ],
        compiler_params=pltpu.CompilerParams(
            collective_id=1, has_side_effects=True, vmem_limit_bytes=48 * 2**20
        ),
        name="merge_parts",
    )(parts, lse)


def pool_kernel(
    groups, per_kv, block, score_scale, first_ref, last_ref, member_ref, q_ref, k_ref, v_ref, o_ref, lse_ref
):
    requests, tree, width = q_ref.shape
    local_kv = k_ref.shape[1] // 128
    per_group = requests // groups
    o_ref[...] = jnp.zeros_like(o_ref)
    lse_ref[...] = jnp.full(lse_ref.shape, NEGATIVE, jnp.float32)

    def attend(owners, first, last):
        count = len(owners) * per_kv * tree
        for kv in range(local_kv):
            keys = slice(kv * 128, (kv + 1) * 128)
            rows = [
                (owner, kv * per_kv + sub) for sub in range(per_kv) for owner in owners
            ]
            query = jnp.concatenate(
                [q_ref[owner, :, head * 128 : (head + 1) * 128] for owner, head in rows], axis=0
            )

            def visit(step, carry):
                run_max, run_sum, run_num = carry
                start = pl.multiple_of(step * block, block)
                scores = (
                    lax.dot_general(
                        query,
                        k_ref[pl.ds(start, block), keys],
                        (((1,), (1,)), ((), ())),
                        preferred_element_type=jnp.float32,
                    )
                    * score_scale
                )
                slots = start + lax.broadcasted_iota(jnp.int32, (1, block), 1)
                scores = jnp.where((slots >= first) & (slots < last), scores, NEGATIVE)
                new_max = jnp.maximum(run_max, jnp.max(scores, axis=1, keepdims=True))
                weights = jnp.exp(scores - new_max)
                factor = jnp.exp(run_max - new_max)
                run_sum = run_sum * factor + jnp.sum(weights, axis=1, keepdims=True)
                run_num = run_num * factor + jnp.dot(
                    weights.astype(jnp.bfloat16),
                    v_ref[pl.ds(start, block), keys],
                    preferred_element_type=jnp.float32,
                )
                return new_max, run_sum, run_num

            run_max, run_sum, run_num = lax.fori_loop(
                first // block,
                (last + block - 1) // block,
                visit,
                (
                    jnp.full((count, 1), NEGATIVE, jnp.float32),
                    jnp.zeros((count, 1), jnp.float32),
                    jnp.zeros((count, 128), jnp.float32),
                ),
            )
            mixed = (run_num / run_sum).astype(o_ref.dtype)
            lse = run_max + jnp.log(run_sum)
            for place, (owner, head) in enumerate(rows):
                part = slice(place * tree, (place + 1) * tree)
                o_ref[owner, :, head * 128 : (head + 1) * 128] = mixed[part]
                lse_ref[owner, :, head : head + 1] = lse[part]

    def group_step(group, unused):
        first, last = first_ref[group], last_ref[group]

        @pl.when(last > first)
        def _():
            attend([member_ref[group * per_group + at] for at in range(per_group)], first, last)

        return unused

    def own_step(owner, unused):
        first, last = first_ref[groups + owner], last_ref[groups + owner]

        @pl.when(last > first)
        def _():
            attend([owner], first, last)

        return unused

    lax.fori_loop(0, groups, group_step, 0)
    lax.fori_loop(0, requests, own_step, 0)


def pool_attention(first, last, members, query, keys, values, groups, per_kv, score_scale):
    requests, tree, width = query.shape
    vmem = pl.BlockSpec(memory_space=pltpu.VMEM)
    smem = pl.BlockSpec(memory_space=pltpu.SMEM)
    return pl.pallas_call(
        functools.partial(pool_kernel, groups, per_kv, min(512, keys.shape[0]), score_scale),
        out_shape=(
            jax.ShapeDtypeStruct(query.shape, jnp.bfloat16),
            jax.ShapeDtypeStruct((requests, tree, 128), jnp.float32),
        ),
        in_specs=[smem, smem, smem, vmem, vmem, vmem],
        out_specs=(vmem, vmem),
        compiler_params=pltpu.CompilerParams(vmem_limit_bytes=48 * 2**20),
        name="pool_attention",
    )(first, last, members, query, keys, values)


def body(
    hidden,
    in_gain,
    w_query,
    key_projection_weight,
    value_projection_weight,
    w_gate,
    w_out,
    q_gain,
    k_gain,
    cache_keys,
    pooled_cache_values,
    prefix_len,
    own_len,
    request_group,
    parents,
    accepted_leaf,
):
    local_req, tree = parents.shape
    groups = prefix_len.shape[0]
    requests = own_len.shape[0]
    head_width = q_gain.shape[0]
    local_heads = w_gate.shape[1]
    local_kv = key_projection_weight.shape[1] // head_width
    per_kv = local_heads // local_kv
    local_tok = hidden.shape[0]
    pool_dev = cache_keys.shape[0]
    seq_index = lax.axis_index("seq")
    score_scale = 1.0 / math.sqrt(head_width)
    full_rows = lax.all_gather(hidden, "kv", axis=1, tiled=True)
    normed = rms_scale(full_rows.astype(jnp.float32), in_gain).astype(jnp.bfloat16)
    reach, depth_f = tree_paths(parents)
    all_reqs = jnp.arange(requests, dtype=jnp.int32)
    my_reqs = seq_index * local_req + jnp.arange(local_req, dtype=jnp.int32)
    my_pick = (my_reqs[:, None] == all_reqs[None, :]).astype(jnp.int32)
    my_group = jnp.sum(my_pick * request_group[None, :], axis=1)
    group_ids = jnp.arange(groups, dtype=jnp.int32)
    group_pick = (my_group[:, None] == group_ids[None, :]).astype(jnp.int32)
    context = jnp.sum(group_pick * prefix_len[None, :], axis=1) + jnp.sum(
        my_pick * own_len[None, :], axis=1
    )
    positions = (context[:, None].astype(jnp.float32) + depth_f).reshape(-1)
    query = jnp.dot(normed, w_query, preferred_element_type=jnp.float32).reshape(
        local_tok, local_heads, head_width
    )
    query = rotate_pairs(rms_scale(query, q_gain), positions).astype(jnp.bfloat16)
    key_new = jnp.dot(normed, key_projection_weight, preferred_element_type=jnp.float32).reshape(
        local_tok, local_kv, head_width
    )
    key_new = rotate_pairs(rms_scale(key_new, k_gain), positions).astype(jnp.bfloat16)
    value_new = (
        jnp.dot(normed, value_projection_weight, preferred_element_type=jnp.float32)
        .astype(jnp.bfloat16)
        .reshape(local_tok, local_kv, head_width)
    )
    gate_logit = jnp.dot(normed, w_gate, preferred_element_type=jnp.float32)
    tree_query = query.reshape(local_req, tree, local_kv, per_kv, head_width)
    tree_keys = key_new.reshape(local_req, tree, local_kv, head_width)
    tree_values = value_new.reshape(local_req, tree, local_kv, head_width)
    tree_scores = (
        jnp.einsum("atkgd,askd->atkgs", tree_query, tree_keys, preferred_element_type=jnp.float32)
        * score_scale
    )
    tree_seen = (reach > 0.5)[:, :, None, None, :]
    tree_scores = jnp.where(tree_seen, tree_scores, NEGATIVE)
    tree_max = jnp.max(tree_scores, axis=-1)
    tree_weights = jnp.where(tree_seen, jnp.exp(tree_scores - tree_max[..., None]), 0.0)
    tree_sum = jnp.sum(tree_weights, axis=-1).reshape(local_tok, local_heads)
    tree_num = jnp.einsum(
        "atkgs,askd->atkgd",
        tree_weights.astype(jnp.bfloat16),
        tree_values,
        preferred_element_type=jnp.float32,
    ).reshape(local_tok, local_heads, head_width)
    tree_max = tree_max.reshape(local_tok, local_heads)
    lengths_all = jnp.concatenate([prefix_len, own_len])
    starts = jnp.cumsum(lengths_all) - lengths_all
    seq_count = requests // local_req
    first = jnp.clip(starts - seq_index * pool_dev, 0, pool_dev)
    last = jnp.clip(starts + lengths_all - seq_index * pool_dev, 0, pool_dev)
    same = (request_group[:, None] == request_group[None, :]) & (all_reqs[None, :] < all_reqs[:, None])
    place = request_group * (requests // groups) + jnp.sum(same.astype(jnp.int32), axis=1)
    members = jnp.sum(
        (place[None, :] == all_reqs[:, None]).astype(jnp.int32) * all_reqs[None, :], axis=1
    )
    gathered = gather_rows(query.reshape(local_tok, local_heads * head_width), seq_count)
    parts, part_lse = pool_attention(
        first,
        last,
        members,
        gathered.reshape(requests, tree, local_heads * head_width),
        cache_keys.reshape(pool_dev, local_kv * head_width),
        pooled_cache_values.reshape(pool_dev, local_kv * head_width),
        groups,
        per_kv,
        score_scale,
    )
    cache_mix, cache_lse = merge_parts(
        parts.reshape(seq_count, local_tok, local_heads * head_width),
        part_lse.reshape(seq_count, local_tok, 128),
        seq_count,
    )
    cache_lse = cache_lse[:, :local_heads]
    final_max = jnp.maximum(cache_lse, tree_max)
    cache_factor = jnp.exp(cache_lse - final_max)
    tree_factor = jnp.exp(tree_max - final_max)
    weight_sum = cache_factor + tree_sum * tree_factor
    mixed = (
        cache_mix.reshape(local_tok, local_heads, head_width) * cache_factor[..., None]
        + tree_num * tree_factor[..., None]
    )
    mixed = mixed / weight_sum[..., None]
    attended = (
        (mixed * jax.nn.sigmoid(gate_logit)[..., None])
        .astype(jnp.bfloat16)
        .reshape(local_tok, local_heads * head_width)
    )
    projected = jnp.dot(attended, w_out, preferred_element_type=jnp.float32)
    layer_part = lax.psum_scatter(
        projected.astype(jnp.bfloat16), "kv", scatter_dimension=1, tiled=True
    ).astype(jnp.float32)
    layer_out = (layer_part + hidden.astype(jnp.float32)).astype(jnp.bfloat16)
    tree_rows = jnp.concatenate(
        [
            key_new.reshape(local_req, tree, local_kv * head_width),
            value_new.reshape(local_req, tree, local_kv * head_width),
        ],
        axis=-1,
    )
    picked = accepted_rows(reach, depth_f, accepted_leaf, tree_rows)
    accepted_keys = picked[:, :, : local_kv * head_width]
    accepted_values = picked[:, :, local_kv * head_width :]
    return (layer_out, accepted_keys, accepted_values)


def solution(mesh):
    in_specs = (
        P("seq", "kv"),
        P(),
        P(None, "kv"),
        P(None, "kv"),
        P(None, "kv"),
        P(None, "kv"),
        P("kv", None),
        P(),
        P(),
        P("seq", "kv", None),
        P("seq", "kv", None),
        P(),
        P(),
        P(),
        P("seq", None),
        P("seq"),
    )
    out_specs = (P("seq", "kv"), P("seq", None, "kv"), P("seq", None, "kv"))
    return jax.shard_map(body, mesh=mesh, in_specs=in_specs, out_specs=out_specs, check_vma=False)
```

```python
import functools
import math

import jax
import jax.numpy as jnp
from jax import lax
from jax.experimental import pallas as pl
from jax.experimental.pallas import tpu as pltpu
from jax.sharding import PartitionSpec as P

EPSILON = 1e-06
ROPE_BASE = 1000000.0
NEGATIVE = -1e30


def rms_scale(values, scales):
    mean_square = jnp.mean(values * values, axis=-1, keepdims=True)
    return values * lax.rsqrt(mean_square + EPSILON) * scales


def rope_tables(positions, head_width):
    half_width = head_width // 2
    freqs = jnp.exp(
        jnp.arange(half_width, dtype=jnp.float32) * (-2.0 * math.log(ROPE_BASE) / head_width)
    )
    angles = positions[:, None] * freqs[None, :]
    cosine = jnp.cos(angles)
    sine = jnp.sin(angles)
    return (
        jnp.concatenate([cosine, cosine], axis=-1),
        jnp.concatenate([-sine, sine], axis=-1),
    )


def tree_paths(parents):
    width = parents.shape[-1]
    nodes = jnp.arange(width, dtype=jnp.int32)
    linked = (parents[:, :, None] == nodes[None, None, :]).astype(jnp.float32)
    identity_mat = jnp.eye(width, dtype=jnp.float32)
    reach = jnp.minimum(identity_mat[None] + linked * (1.0 - identity_mat[None]), 1.0)
    for squaring in range(max(1, (width - 1).bit_length())):
        reach = jnp.minimum(
            jnp.einsum("mij,mjk->mik", reach, reach, precision=lax.Precision.HIGHEST), 1.0
        )
    depth_f = jnp.sum(reach, axis=-1) - 1.0
    return (reach, depth_f)


def accepted_rows(reach, depth_f, leaves, tree_rows):
    width = reach.shape[-1]
    nodes = jnp.arange(width, dtype=jnp.int32)
    leaf_pick = (leaves[:, None] == nodes[None, :]).astype(jnp.float32)
    on_path = jnp.einsum("mi,mij->mj", leaf_pick, reach, precision=lax.Precision.HIGHEST)
    levels = (depth_f[:, None, :] == nodes.astype(jnp.float32)[None, :, None]).astype(jnp.float32)
    select = levels * on_path[:, None, :]
    return jnp.einsum(
        "mdj,mjc->mdc", select, tree_rows.astype(jnp.float32), precision=lax.Precision.HIGHEST
    ).astype(jnp.bfloat16)


def lowest(distance):
    return distance & -distance


def flip(index, distance):
    out = index
    bit = 1
    while bit <= distance:
        if distance & bit:
            out = out + bit * (1 - 2 * ((index // bit) % 2))
        bit *= 2
    return out


def one_bits(count):
    bits = []
    bit = 1
    while bit < count:
        bits.append(bit)
        bit *= 2
    return bits


def greet(me, count, kv, kv_count):
    barrier = pltpu.get_barrier_semaphore()
    bits = one_bits(count)
    for bit in bits:
        pl.semaphore_signal(barrier, inc=1, device_id={"seq": flip(me, bit)})
    for hop in range(1, kv_count):
        pl.semaphore_signal(barrier, inc=1, device_id={"kv": (kv + hop) % kv_count})
    pl.semaphore_wait(barrier, len(bits) + kv_count - 1)


def layer_kernel(
    count,
    kv_count,
    score_scale,
    hidden_ref,
    in_gain_ref,
    w_query_ref,
    w_key_ref,
    w_value_ref,
    w_gate_ref,
    q_gain_ref,
    k_gain_ref,
    cos_ref,
    sin_ref,
    seen_ref,
    all_ref,
    key_ref,
    value_ref,
    tree_ref,
    tree_lse_ref,
    gate_ref,
    wide,
    w_query,
    w_key,
    w_value,
    load_sem,
    wide_send,
    wide_recv,
    send_sem,
    recv_sem,
):
    me = lax.axis_index("seq")
    kv = lax.axis_index("kv")
    loads = [
        pltpu.make_async_copy(source, target, load_sem.at[which])
        for which, (source, target) in enumerate(
            [(w_query_ref, w_query), (w_key_ref, w_key), (w_value_ref, w_value)]
        )
    ]
    for load in loads:
        load.start()
    wide[kv] = hidden_ref[...]
    greet(me, count, kv, kv_count)

    def wide_message(hop, owner):
        return pltpu.make_async_remote_copy(
            src_ref=wide.at[owner],
            dst_ref=wide.at[owner],
            send_sem=wide_send.at[hop],
            recv_sem=wide_recv.at[hop],
            device_id={"kv": (kv + hop) % kv_count},
        )

    wide_sent = [wide_message(hop, kv) for hop in range(1, kv_count)]
    for copy in wide_sent:
        copy.start()
    for hop in range(1, kv_count):
        wide_message(hop, (kv + kv_count - hop) % kv_count).wait_recv()
    rows = jnp.concatenate([wide[at] for at in range(kv_count)], axis=1).astype(jnp.float32)
    normed = rms_scale(rows, in_gain_ref[...]).astype(jnp.bfloat16)

    def rotated(values, gain_ref):
        values = rms_scale(values, gain_ref[...])
        return (values * cos_ref[...] + pltpu.roll(values, 64, 1) * sin_ref[...]).astype(jnp.bfloat16)

    loads[0].wait()
    query = jnp.dot(normed, w_query[...], preferred_element_type=jnp.float32)
    heads = query.shape[1] // 128
    queries = [rotated(query[:, h * 128 : (h + 1) * 128], q_gain_ref) for h in range(heads)]
    for head in range(heads):
        all_ref[me, :, head * 128 : (head + 1) * 128] = queries[head]

    def message(distance, owner):
        return pltpu.make_async_remote_copy(
            src_ref=all_ref.at[owner],
            dst_ref=all_ref.at[owner],
            send_sem=send_sem.at[distance],
            recv_sem=recv_sem.at[distance],
            device_id={"seq": flip(me, lowest(distance))},
        )

    sent = []

    def hand_on(distance):
        owner = flip(me, distance)
        if distance:
            message(distance, owner).wait_recv()
        for bit in reversed(one_bits(lowest(distance) if distance else count)):
            copy = message(distance | bit, owner)
            copy.start()
            sent.append(copy)

    hand_on(0)
    local_kv = key_ref.shape[1] // 128
    per_kv = heads // local_kv
    tokens = hidden_ref.shape[0]

    def keys_work():
        loads[1].wait()
        key = jnp.dot(normed, w_key[...], preferred_element_type=jnp.float32)
        for at in range(local_kv):
            cols = slice(at * 128, (at + 1) * 128)
            key_ref[:, cols] = rotated(key[:, cols], k_gain_ref)

    def values_work():
        loads[2].wait()
        value_ref[...] = jnp.dot(
            normed, w_value[...], preferred_element_type=jnp.float32
        ).astype(jnp.bfloat16)
        gate_ref[...] = jax.nn.sigmoid(
            jnp.dot(normed, w_gate_ref[...], preferred_element_type=jnp.float32)
        )
        tree_lse_ref[...] = jnp.zeros(tree_lse_ref.shape, jnp.float32)

    def tree_work(at):
        cols = slice(at * 128, (at + 1) * 128)
        stacked = jnp.concatenate(queries[at * per_kv : (at + 1) * per_kv], axis=0)
        scores = (
            lax.dot_general(
                stacked,
                key_ref[:, cols],
                (((1,), (1,)), ((), ())),
                preferred_element_type=jnp.float32,
            )
            * score_scale
        )
        seen = jnp.concatenate([seen_ref[...]] * per_kv, axis=0) > 0.5
        scores = jnp.where(seen, scores, NEGATIVE)
        top = jnp.max(scores, axis=1, keepdims=True)
        weights = jnp.where(seen, jnp.exp(scores - top), 0.0)
        total = jnp.sum(weights, axis=1, keepdims=True)
        mixed = (
            jnp.dot(
                weights.astype(jnp.bfloat16), value_ref[:, cols], preferred_element_type=jnp.float32
            )
            / total
        )
        lse = top + jnp.log(total)
        for sub in range(per_kv):
            head = at * per_kv + sub
            part = slice(sub * tokens, (sub + 1) * tokens)
            tree_ref[:, head * 128 : (head + 1) * 128] = mixed[part]
            tree_lse_ref[:, head : head + 1] = lse[part]

    work = [keys_work, values_work] + [functools.partial(tree_work, at) for at in range(local_kv)]
    order = sorted(range(2, count, 2), key=lambda d: (-lowest(d), d))
    for distance in order:
        if work:
            work.pop(0)()
        hand_on(distance)
    for rest in work:
        rest()
    for distance in range(1, count, 2):
        hand_on(distance)
    for copy in wide_sent + sent:
        copy.wait_send()


def layer_front(
    hidden, in_gain, w_query, w_key, w_value, w_gate, q_gain, k_gain, cosine, sine, seen, count, kv_count, score_scale
):
    tokens = hidden.shape[0]
    width = w_query.shape[1]
    vmem = pl.BlockSpec(memory_space=pltpu.VMEM)
    anywhere = pl.BlockSpec(memory_space=pl.ANY)
    return pl.pallas_call(
        functools.partial(layer_kernel, count, kv_count, score_scale),
        out_shape=(
            jax.ShapeDtypeStruct((count, tokens, width), jnp.bfloat16),
            jax.ShapeDtypeStruct((tokens, w_key.shape[1]), jnp.bfloat16),
            jax.ShapeDtypeStruct((tokens, w_value.shape[1]), jnp.bfloat16),
            jax.ShapeDtypeStruct((tokens, width), jnp.float32),
            jax.ShapeDtypeStruct((tokens, 128), jnp.float32),
            jax.ShapeDtypeStruct((tokens, w_gate.shape[1]), jnp.float32),
        ),
        in_specs=[vmem, vmem, anywhere, anywhere, anywhere] + [vmem] * 6,
        out_specs=(vmem,) * 6,
        scratch_shapes=[
            pltpu.VMEM((kv_count,) + hidden.shape, hidden.dtype),
            pltpu.VMEM(w_query.shape, w_query.dtype),
            pltpu.VMEM(w_key.shape, w_key.dtype),
            pltpu.VMEM(w_value.shape, w_value.dtype),
            pltpu.SemaphoreType.DMA((3,)),
            pltpu.SemaphoreType.DMA((kv_count,)),
            pltpu.SemaphoreType.DMA((kv_count,)),
            pltpu.SemaphoreType.DMA((count,)),
            pltpu.SemaphoreType.DMA((count,)),
        ],
        compiler_params=pltpu.CompilerParams(
            collective_id=0, has_side_effects=True, vmem_limit_bytes=48 * 2**20
        ),
        name="layer_front",
    )(hidden, in_gain[None], w_query, w_key, w_value, w_gate, q_gain[None], k_gain[None], cosine, sine, seen)


def merge_kernel(
    count,
    kv_count,
    part_ref,
    lse_ref,
    tree_ref,
    tree_lse_ref,
    gate_ref,
    w_out_ref,
    hidden_ref,
    out_ref,
    got,
    got_lse,
    held,
    held_lse,
    w_out,
    attended,
    outgoing,
    arrived,
    send_sem,
    recv_sem,
    load_sem,
    out_send,
    out_recv,
):
    me = lax.axis_index("seq")
    kv = lax.axis_index("kv")
    heads = part_ref.shape[2] // 128
    load = pltpu.make_async_copy(w_out_ref, w_out, load_sem)
    load.start()
    greet(me, count, kv, kv_count)

    def messages(distance):
        owner = flip(me, distance)
        if distance % 2:
            sources = (part_ref.at[owner], lse_ref.at[owner])
        else:
            sources = (held.at[distance // 2], held_lse.at[distance // 2])
        return [
            pltpu.make_async_remote_copy(
                src_ref=source,
                dst_ref=target.at[distance],
                send_sem=send_sem.at[which, distance],
                recv_sem=recv_sem.at[which, distance],
                device_id={"seq": flip(me, lowest(distance))},
            )
            for which, (source, target) in enumerate(zip(sources, (got, got_lse)))
        ]

    sent = []

    def send(distance):
        for copy in messages(distance):
            copy.start()
            sent.append(copy)

    for distance in sorted(range(1, count, 2), reverse=True):
        send(distance)
    evens = sorted(range(2, count, 2), key=lambda d: (lowest(d), -d))
    for distance in evens + [0]:
        owner = flip(me, distance)
        incoming = [distance | bit for bit in one_bits(lowest(distance) if distance else count)]
        for message in incoming:
            for copy in messages(message):
                copy.wait_recv()
        levels = [lse_ref[owner]] + [got_lse[message] for message in incoming]
        if not distance:
            levels.append(tree_lse_ref[...])
        top = functools.reduce(jnp.maximum, levels)
        shares = [jnp.exp(level - top) for level in levels]
        total = functools.reduce(jnp.add, shares)
        inverse = 1.0 / total
        shares = [share * inverse for share in shares]
        if distance:
            held_lse[distance // 2] = top + jnp.log(total)
        for head in range(heads):
            cols = slice(head * 128, (head + 1) * 128)
            pieces = [part_ref[owner, :, cols]] + [got[message, :, cols] for message in incoming]
            if not distance:
                pieces.append(tree_ref[:, cols])
            mixed = functools.reduce(
                jnp.add,
                [
                    piece.astype(jnp.float32) * share[:, head : head + 1]
                    for piece, share in zip(pieces, shares)
                ],
            )
            if distance:
                held[distance // 2, :, cols] = mixed.astype(held.dtype)
            else:
                attended[:, cols] = (mixed * gate_ref[:, head : head + 1]).astype(jnp.bfloat16)
        if distance:
            send(distance)
    load.wait()
    width = out_ref.shape[1]

    def projected(target):
        cols = pl.ds(pl.multiple_of(target * width, 128), width)
        return jnp.dot(attended[...], w_out[:, cols], preferred_element_type=jnp.float32)

    def out_message(hop):
        return pltpu.make_async_remote_copy(
            src_ref=outgoing.at[hop],
            dst_ref=arrived.at[hop],
            send_sem=out_send.at[hop],
            recv_sem=out_recv.at[hop],
            device_id={"kv": (kv + hop) % kv_count},
        )

    for hop in range(1, kv_count):
        outgoing[hop] = projected((kv + hop) % kv_count).astype(jnp.bfloat16)
        copy = out_message(hop)
        copy.start()
        sent.append(copy)
    total = projected(kv)
    for hop in range(1, kv_count):
        out_message(hop).wait_recv()
        total = total + arrived[hop].astype(jnp.float32)
    out_ref[...] = (total + hidden_ref[...].astype(jnp.float32)).astype(jnp.bfloat16)
    for copy in sent:
        copy.wait_send()


def merge_parts(parts, lse, tree_mix, tree_lse, gate, w_out, hidden, count, kv_count):
    rows, width = parts.shape[1:]
    lanes = lse.shape[2]
    half = max(1, count // 2)
    vmem = pl.BlockSpec(memory_space=pltpu.VMEM)
    return pl.pallas_call(
        functools.partial(merge_kernel, count, kv_count),
        out_shape=jax.ShapeDtypeStruct(hidden.shape, jnp.bfloat16),
        in_specs=[vmem] * 5 + [pl.BlockSpec(memory_space=pl.ANY), vmem],
        out_specs=vmem,
        scratch_shapes=[
            pltpu.VMEM((count, rows, width), parts.dtype),
            pltpu.VMEM((count, rows, lanes), jnp.float32),
            pltpu.VMEM((half, rows, width), parts.dtype),
            pltpu.VMEM((half, rows, lanes), jnp.float32),
            pltpu.VMEM(w_out.shape, w_out.dtype),
            pltpu.VMEM((rows, width), jnp.bfloat16),
            pltpu.VMEM((kv_count,) + hidden.shape, jnp.bfloat16),
            pltpu.VMEM((kv_count,) + hidden.shape, jnp.bfloat16),
            pltpu.SemaphoreType.DMA((2, count)),
            pltpu.SemaphoreType.DMA((2, count)),
            pltpu.SemaphoreType.DMA,
            pltpu.SemaphoreType.DMA((kv_count,)),
            pltpu.SemaphoreType.DMA((kv_count,)),
        ],
        compiler_params=pltpu.CompilerParams(
            collective_id=1, has_side_effects=True, vmem_limit_bytes=48 * 2**20
        ),
        name="merge_parts",
    )(parts, lse, tree_mix, tree_lse, gate, w_out, hidden)


def pool_kernel(
    groups, per_kv, block, score_scale, first_ref, last_ref, member_ref, q_ref, k_ref, v_ref, o_ref, lse_ref
):
    requests, tree, width = q_ref.shape
    local_kv = k_ref.shape[1] // 128
    per_group = requests // groups
    o_ref[...] = jnp.zeros_like(o_ref)
    lse_ref[...] = jnp.full(lse_ref.shape, NEGATIVE, jnp.float32)

    def attend(owners, first, last):
        count = len(owners) * per_kv * tree
        for kv in range(local_kv):
            keys = slice(kv * 128, (kv + 1) * 128)
            rows = [
                (owner, kv * per_kv + sub) for sub in range(per_kv) for owner in owners
            ]
            query = jnp.concatenate(
                [q_ref[owner, :, head * 128 : (head + 1) * 128] for owner, head in rows], axis=0
            )

            def visit(step, carry):
                run_max, run_sum, run_num = carry
                start = pl.multiple_of(step * block, block)
                scores = (
                    lax.dot_general(
                        query,
                        k_ref[pl.ds(start, block), keys],
                        (((1,), (1,)), ((), ())),
                        preferred_element_type=jnp.float32,
                    )
                    * score_scale
                )
                slots = start + lax.broadcasted_iota(jnp.int32, (1, block), 1)
                scores = jnp.where((slots >= first) & (slots < last), scores, NEGATIVE)
                new_max = jnp.maximum(run_max, jnp.max(scores, axis=1, keepdims=True))
                weights = jnp.exp(scores - new_max)
                factor = jnp.exp(run_max - new_max)
                run_sum = run_sum * factor + jnp.sum(weights, axis=1, keepdims=True)
                run_num = run_num * factor + jnp.dot(
                    weights.astype(jnp.bfloat16),
                    v_ref[pl.ds(start, block), keys],
                    preferred_element_type=jnp.float32,
                )
                return new_max, run_sum, run_num

            run_max, run_sum, run_num = lax.fori_loop(
                first // block,
                (last + block - 1) // block,
                visit,
                (
                    jnp.full((count, 1), NEGATIVE, jnp.float32),
                    jnp.zeros((count, 1), jnp.float32),
                    jnp.zeros((count, 128), jnp.float32),
                ),
            )
            mixed = (run_num / run_sum).astype(o_ref.dtype)
            lse = run_max + jnp.log(run_sum)
            for place, (owner, head) in enumerate(rows):
                part = slice(place * tree, (place + 1) * tree)
                o_ref[owner, :, head * 128 : (head + 1) * 128] = mixed[part]
                lse_ref[owner, :, head : head + 1] = lse[part]

    def group_step(group, unused):
        first, last = first_ref[group], last_ref[group]

        @pl.when(last > first)
        def _():
            attend([member_ref[group * per_group + at] for at in range(per_group)], first, last)

        return unused

    def own_step(owner, unused):
        first, last = first_ref[groups + owner], last_ref[groups + owner]

        @pl.when(last > first)
        def _():
            attend([owner], first, last)

        return unused

    lax.fori_loop(0, groups, group_step, 0)
    lax.fori_loop(0, requests, own_step, 0)


def pool_attention(first, last, members, query, keys, values, groups, per_kv, score_scale):
    requests, tree, width = query.shape
    vmem = pl.BlockSpec(memory_space=pltpu.VMEM)
    smem = pl.BlockSpec(memory_space=pltpu.SMEM)
    return pl.pallas_call(
        functools.partial(pool_kernel, groups, per_kv, min(512, keys.shape[0]), score_scale),
        out_shape=(
            jax.ShapeDtypeStruct(query.shape, jnp.bfloat16),
            jax.ShapeDtypeStruct((requests, tree, 128), jnp.float32),
        ),
        in_specs=[smem, smem, smem, vmem, vmem, vmem],
        out_specs=(vmem, vmem),
        compiler_params=pltpu.CompilerParams(vmem_limit_bytes=48 * 2**20),
        name="pool_attention",
    )(first, last, members, query, keys, values)


def body(
    hidden,
    in_gain,
    w_query,
    key_projection_weight,
    value_projection_weight,
    w_gate,
    w_out,
    q_gain,
    k_gain,
    cache_keys,
    pooled_cache_values,
    prefix_len,
    own_len,
    request_group,
    parents,
    accepted_leaf,
):
    local_req, tree = parents.shape
    groups = prefix_len.shape[0]
    requests = own_len.shape[0]
    head_width = q_gain.shape[0]
    local_heads = w_gate.shape[1]
    local_kv = key_projection_weight.shape[1] // head_width
    per_kv = local_heads // local_kv
    local_tok = hidden.shape[0]
    pool_dev = cache_keys.shape[0]
    seq_index = lax.axis_index("seq")
    score_scale = 1.0 / math.sqrt(head_width)
    seq_count = requests // local_req
    kv_count = in_gain.shape[0] // hidden.shape[1]
    reach, depth_f = tree_paths(parents)
    all_reqs = jnp.arange(requests, dtype=jnp.int32)
    my_reqs = seq_index * local_req + jnp.arange(local_req, dtype=jnp.int32)
    my_pick = (my_reqs[:, None] == all_reqs[None, :]).astype(jnp.int32)
    my_group = jnp.sum(my_pick * request_group[None, :], axis=1)
    group_ids = jnp.arange(groups, dtype=jnp.int32)
    group_pick = (my_group[:, None] == group_ids[None, :]).astype(jnp.int32)
    context = jnp.sum(group_pick * prefix_len[None, :], axis=1) + jnp.sum(
        my_pick * own_len[None, :], axis=1
    )
    positions = (context[:, None].astype(jnp.float32) + depth_f).reshape(-1)
    cosine, sine = rope_tables(positions, head_width)
    seen = (reach[:, :, None, :] * jnp.eye(local_req, dtype=jnp.float32)[:, None, :, None]).reshape(
        local_tok, local_tok
    )
    gathered, key_new, value_new, tree_mix, tree_lse, gate = layer_front(
        hidden,
        in_gain,
        w_query,
        key_projection_weight,
        value_projection_weight,
        w_gate,
        q_gain,
        k_gain,
        cosine,
        sine,
        seen,
        seq_count,
        kv_count,
        score_scale,
    )
    lengths_all = jnp.concatenate([prefix_len, own_len])
    starts = jnp.cumsum(lengths_all) - lengths_all
    first = jnp.clip(starts - seq_index * pool_dev, 0, pool_dev)
    last = jnp.clip(starts + lengths_all - seq_index * pool_dev, 0, pool_dev)
    same = (request_group[:, None] == request_group[None, :]) & (all_reqs[None, :] < all_reqs[:, None])
    place = request_group * (requests // groups) + jnp.sum(same.astype(jnp.int32), axis=1)
    members = jnp.sum(
        (place[None, :] == all_reqs[:, None]).astype(jnp.int32) * all_reqs[None, :], axis=1
    )
    parts, part_lse = pool_attention(
        first,
        last,
        members,
        gathered.reshape(requests, tree, local_heads * head_width),
        cache_keys.reshape(pool_dev, local_kv * head_width),
        pooled_cache_values.reshape(pool_dev, local_kv * head_width),
        groups,
        per_kv,
        score_scale,
    )
    layer_out = merge_parts(
        parts.reshape(seq_count, local_tok, local_heads * head_width),
        part_lse.reshape(seq_count, local_tok, 128),
        tree_mix,
        tree_lse,
        gate,
        w_out,
        hidden,
        seq_count,
        kv_count,
    )
    tree_rows = jnp.concatenate(
        [
            key_new.reshape(local_req, tree, local_kv * head_width),
            value_new.reshape(local_req, tree, local_kv * head_width),
        ],
        axis=-1,
    )
    picked = accepted_rows(reach, depth_f, accepted_leaf, tree_rows)
    accepted_keys = picked[:, :, : local_kv * head_width]
    accepted_values = picked[:, :, local_kv * head_width :]
    return (layer_out, accepted_keys, accepted_values)


def solution(mesh):
    in_specs = (
        P("seq", "kv"),
        P(),
        P(None, "kv"),
        P(None, "kv"),
        P(None, "kv"),
        P(None, "kv"),
        P("kv", None),
        P(),
        P(),
        P("seq", "kv", None),
        P("seq", "kv", None),
        P(),
        P(),
        P(),
        P("seq", None),
        P("seq"),
    )
    out_specs = (P("seq", "kv"), P("seq", None, "kv"), P("seq", None, "kv"))
    return jax.shard_map(body, mesh=mesh, in_specs=in_specs, out_specs=out_specs, check_vma=False)
```

```python
import functools
import math

import jax
import jax.numpy as jnp
from jax import lax
from jax.experimental import pallas as pl
from jax.experimental.pallas import tpu as pltpu
from jax.sharding import PartitionSpec as P

EPSILON = 1e-06
ROPE_BASE = 1000000.0
NEGATIVE = -1e30


def rms_scale(values, scales):
    mean_square = jnp.mean(values * values, axis=-1, keepdims=True)
    return values * lax.rsqrt(mean_square + EPSILON) * scales


def rope_tables(positions, head_width):
    half_width = head_width // 2
    freqs = jnp.exp(
        jnp.arange(half_width, dtype=jnp.float32) * (-2.0 * math.log(ROPE_BASE) / head_width)
    )
    angles = positions[:, None] * freqs[None, :]
    cosine = jnp.cos(angles)
    sine = jnp.sin(angles)
    return (
        jnp.concatenate([cosine, cosine], axis=-1),
        jnp.concatenate([-sine, sine], axis=-1),
    )


def tree_paths(parents):
    width = parents.shape[-1]
    nodes = jnp.arange(width, dtype=jnp.int32)
    linked = (parents[:, :, None] == nodes[None, None, :]).astype(jnp.float32)
    identity_mat = jnp.eye(width, dtype=jnp.float32)
    reach = jnp.minimum(identity_mat[None] + linked * (1.0 - identity_mat[None]), 1.0)
    for squaring in range(max(1, (width - 1).bit_length())):
        reach = jnp.minimum(
            jnp.einsum("mij,mjk->mik", reach, reach, precision=lax.Precision.HIGHEST), 1.0
        )
    depth_f = jnp.sum(reach, axis=-1) - 1.0
    return (reach, depth_f)


def accepted_rows(reach, depth_f, leaves, tree_rows):
    width = reach.shape[-1]
    nodes = jnp.arange(width, dtype=jnp.int32)
    leaf_pick = (leaves[:, None] == nodes[None, :]).astype(jnp.float32)
    on_path = jnp.einsum("mi,mij->mj", leaf_pick, reach, precision=lax.Precision.HIGHEST)
    levels = (depth_f[:, None, :] == nodes.astype(jnp.float32)[None, :, None]).astype(jnp.float32)
    select = levels * on_path[:, None, :]
    return jnp.einsum(
        "mdj,mjc->mdc", select, tree_rows.astype(jnp.float32), precision=lax.Precision.HIGHEST
    ).astype(jnp.bfloat16)


def lowest(distance):
    return distance & -distance


def flip(index, distance):
    out = index
    bit = 1
    while bit <= distance:
        if distance & bit:
            out = out + bit * (1 - 2 * ((index // bit) % 2))
        bit *= 2
    return out


def one_bits(count):
    bits = []
    bit = 1
    while bit < count:
        bits.append(bit)
        bit *= 2
    return bits


def greet(me, count, kv, kv_count):
    barrier = pltpu.get_barrier_semaphore()
    bits = one_bits(count)
    for bit in bits:
        pl.semaphore_signal(barrier, inc=1, device_id={"seq": flip(me, bit)})
    for hop in range(1, kv_count):
        pl.semaphore_signal(barrier, inc=1, device_id={"kv": (kv + hop) % kv_count})
    pl.semaphore_wait(barrier, len(bits) + kv_count - 1)


def layer_kernel(
    count,
    kv_count,
    score_scale,
    hidden_ref,
    in_gain_ref,
    w_query_ref,
    w_key_ref,
    w_value_ref,
    w_gate_ref,
    q_gain_ref,
    k_gain_ref,
    cos_ref,
    sin_ref,
    seen_ref,
    all_ref,
    key_ref,
    value_ref,
    tree_ref,
    tree_lse_ref,
    gate_ref,
    wide,
    w_query,
    w_key,
    w_value,
    w_gate,
    in_gain,
    q_gain,
    k_gain,
    load_sem,
    wide_send,
    wide_recv,
    send_sem,
    recv_sem,
):
    me = lax.axis_index("seq")
    kv = lax.axis_index("kv")
    loads = [
        pltpu.make_async_copy(source, target, load_sem.at[which])
        for which, (source, target) in enumerate(
            [
                (hidden_ref, wide.at[kv]),
                (in_gain_ref, in_gain),
                (q_gain_ref, q_gain),
                (k_gain_ref, k_gain),
                (w_query_ref, w_query),
                (w_key_ref, w_key),
                (w_value_ref, w_value),
                (w_gate_ref, w_gate),
            ]
        )
    ]
    for load in loads:
        load.start()
    loads[0].wait()
    greet(me, count, kv, kv_count)

    def wide_message(hop, owner):
        return pltpu.make_async_remote_copy(
            src_ref=wide.at[owner],
            dst_ref=wide.at[owner],
            send_sem=wide_send.at[hop],
            recv_sem=wide_recv.at[hop],
            device_id={"kv": (kv + hop) % kv_count},
        )

    wide_sent = [wide_message(hop, kv) for hop in range(1, kv_count)]
    for copy in wide_sent:
        copy.start()
    for hop in range(1, kv_count):
        wide_message(hop, (kv + kv_count - hop) % kv_count).wait_recv()
    rows = jnp.concatenate([wide[at] for at in range(kv_count)], axis=1).astype(jnp.float32)
    for load in loads[1:4]:
        load.wait()
    normed = rms_scale(rows, in_gain[...]).astype(jnp.bfloat16)

    def rotated(values, gain):
        values = rms_scale(values, gain[...])
        return (values * cos_ref[...] + pltpu.roll(values, 64, 1) * sin_ref[...]).astype(jnp.bfloat16)

    loads[4].wait()
    query = jnp.dot(normed, w_query[...], preferred_element_type=jnp.float32)
    heads = query.shape[1] // 128
    queries = [rotated(query[:, h * 128 : (h + 1) * 128], q_gain) for h in range(heads)]
    for head in range(heads):
        all_ref[me, :, head * 128 : (head + 1) * 128] = queries[head]

    def message(distance, owner):
        return pltpu.make_async_remote_copy(
            src_ref=all_ref.at[owner],
            dst_ref=all_ref.at[owner],
            send_sem=send_sem.at[distance],
            recv_sem=recv_sem.at[distance],
            device_id={"seq": flip(me, lowest(distance))},
        )

    sent = []

    def hand_on(distance):
        owner = flip(me, distance)
        if distance:
            message(distance, owner).wait_recv()
        for bit in reversed(one_bits(lowest(distance) if distance else count)):
            copy = message(distance | bit, owner)
            copy.start()
            sent.append(copy)

    hand_on(0)
    local_kv = key_ref.shape[1] // 128
    per_kv = heads // local_kv
    tokens = hidden_ref.shape[0]

    def keys_work():
        loads[5].wait()
        key = jnp.dot(normed, w_key[...], preferred_element_type=jnp.float32)
        for at in range(local_kv):
            cols = slice(at * 128, (at + 1) * 128)
            key_ref[:, cols] = rotated(key[:, cols], k_gain)

    def values_work():
        loads[6].wait()
        loads[7].wait()
        value_ref[...] = jnp.dot(
            normed, w_value[...], preferred_element_type=jnp.float32
        ).astype(jnp.bfloat16)
        gate_ref[...] = jax.nn.sigmoid(
            lax.dot_general(
                normed, w_gate[...], (((1,), (1,)), ((), ())), preferred_element_type=jnp.float32
            )
        )
        tree_lse_ref[...] = jnp.zeros(tree_lse_ref.shape, jnp.float32)

    def tree_work(at):
        cols = slice(at * 128, (at + 1) * 128)
        stacked = jnp.concatenate(queries[at * per_kv : (at + 1) * per_kv], axis=0)
        scores = (
            lax.dot_general(
                stacked,
                key_ref[:, cols],
                (((1,), (1,)), ((), ())),
                preferred_element_type=jnp.float32,
            )
            * score_scale
        )
        seen = jnp.concatenate([seen_ref[...]] * per_kv, axis=0) > 0.5
        scores = jnp.where(seen, scores, NEGATIVE)
        top = jnp.max(scores, axis=1, keepdims=True)
        weights = jnp.where(seen, jnp.exp(scores - top), 0.0)
        total = jnp.sum(weights, axis=1, keepdims=True)
        mixed = (
            jnp.dot(
                weights.astype(jnp.bfloat16), value_ref[:, cols], preferred_element_type=jnp.float32
            )
            / total
        )
        lse = top + jnp.log(total)
        for sub in range(per_kv):
            head = at * per_kv + sub
            part = slice(sub * tokens, (sub + 1) * tokens)
            tree_ref[:, head * 128 : (head + 1) * 128] = mixed[part]
            tree_lse_ref[:, head : head + 1] = lse[part]

    work = [keys_work, values_work] + [functools.partial(tree_work, at) for at in range(local_kv)]
    order = sorted(range(2, count, 2), key=lambda d: (-lowest(d), d))
    for distance in order:
        if work:
            work.pop(0)()
        hand_on(distance)
    for rest in work:
        rest()
    for distance in range(1, count, 2):
        hand_on(distance)
    for copy in wide_sent + sent:
        copy.wait_send()


def layer_front(
    hidden, in_gain, w_query, w_key, w_value, w_gate, q_gain, k_gain, cosine, sine, seen, count, kv_count, score_scale
):
    tokens = hidden.shape[0]
    width = w_query.shape[1]
    vmem = pl.BlockSpec(memory_space=pltpu.VMEM)
    hbm = pl.BlockSpec(memory_space=pltpu.HBM)
    return pl.pallas_call(
        functools.partial(layer_kernel, count, kv_count, score_scale),
        out_shape=(
            jax.ShapeDtypeStruct((count, tokens, width), jnp.bfloat16),
            jax.ShapeDtypeStruct((tokens, w_key.shape[1]), jnp.bfloat16),
            jax.ShapeDtypeStruct((tokens, w_value.shape[1]), jnp.bfloat16),
            jax.ShapeDtypeStruct((tokens, width), jnp.float32),
            jax.ShapeDtypeStruct((tokens, 128), jnp.float32),
            jax.ShapeDtypeStruct((tokens, w_gate.shape[0]), jnp.float32),
        ),
        in_specs=[hbm] * 8 + [vmem] * 3,
        out_specs=(vmem,) * 6,
        scratch_shapes=[
            pltpu.VMEM((kv_count,) + hidden.shape, hidden.dtype),
            pltpu.VMEM(w_query.shape, w_query.dtype),
            pltpu.VMEM(w_key.shape, w_key.dtype),
            pltpu.VMEM(w_value.shape, w_value.dtype),
            pltpu.VMEM(w_gate.shape, w_gate.dtype),
            pltpu.VMEM((1, in_gain.shape[0]), jnp.float32),
            pltpu.VMEM((1, 128), jnp.float32),
            pltpu.VMEM((1, 128), jnp.float32),
            pltpu.SemaphoreType.DMA((8,)),
            pltpu.SemaphoreType.DMA((kv_count,)),
            pltpu.SemaphoreType.DMA((kv_count,)),
            pltpu.SemaphoreType.DMA((count,)),
            pltpu.SemaphoreType.DMA((count,)),
        ],
        compiler_params=pltpu.CompilerParams(
            collective_id=0, has_side_effects=True, vmem_limit_bytes=48 * 2**20
        ),
        name="layer_front",
    )(hidden, in_gain[None], w_query, w_key, w_value, w_gate, q_gain[None], k_gain[None], cosine, sine, seen)


def merge_kernel(
    count,
    kv_count,
    part_ref,
    lse_ref,
    tree_ref,
    tree_lse_ref,
    gate_ref,
    w_out_ref,
    hidden_ref,
    out_ref,
    got,
    got_lse,
    mine_lse,
    held,
    held_lse,
    w_out,
    attended,
    outgoing,
    arrived,
    send_sem,
    recv_sem,
    load_sem,
    out_send,
    out_recv,
):
    me = lax.axis_index("seq")
    kv = lax.axis_index("kv")
    heads = part_ref.shape[2] // 128
    load = pltpu.make_async_copy(w_out_ref, w_out, load_sem)
    load.start()
    rows = part_ref.shape[1]

    def across(level):
        turned = jnp.transpose(level)[:8]
        return jnp.concatenate([turned] * (128 // rows), axis=1)

    for distance in range(count):
        mine_lse[distance] = across(lse_ref[flip(me, distance)])
    greet(me, count, kv, kv_count)

    def messages(distance):
        owner = flip(me, distance)
        if distance % 2:
            sources = (part_ref.at[owner], mine_lse.at[distance])
        else:
            sources = (held.at[distance // 2], held_lse.at[distance // 2])
        return [
            pltpu.make_async_remote_copy(
                src_ref=source,
                dst_ref=target.at[distance],
                send_sem=send_sem.at[which, distance],
                recv_sem=recv_sem.at[which, distance],
                device_id={"seq": flip(me, lowest(distance))},
            )
            for which, (source, target) in enumerate(zip(sources, (got, got_lse)))
        ]

    sent = []

    def send(distance):
        for copy in messages(distance):
            copy.start()
            sent.append(copy)

    for distance in sorted(range(1, count, 2), reverse=True):
        send(distance)
    evens = sorted(range(2, count, 2), key=lambda d: (lowest(d), -d))
    for distance in evens + [0]:
        owner = flip(me, distance)
        incoming = [distance | bit for bit in one_bits(lowest(distance) if distance else count)]
        for message in incoming:
            for copy in messages(message):
                copy.wait_recv()
        levels = [mine_lse[distance]] + [got_lse[message] for message in incoming]
        if not distance:
            levels.append(across(tree_lse_ref[...]))
        top = functools.reduce(jnp.maximum, levels)
        shares = [jnp.exp(level - top) for level in levels]
        total = functools.reduce(jnp.add, shares)
        inverse = 1.0 / total
        shares = [jnp.transpose(share * inverse)[:rows] for share in shares]
        if distance:
            held_lse[distance // 2] = top + jnp.log(total)
        for head in range(heads):
            cols = slice(head * 128, (head + 1) * 128)
            pieces = [part_ref[owner, :, cols]] + [got[message, :, cols] for message in incoming]
            if not distance:
                pieces.append(tree_ref[:, cols])
            mixed = functools.reduce(
                jnp.add,
                [
                    piece.astype(jnp.float32) * share[:, head : head + 1]
                    for piece, share in zip(pieces, shares)
                ],
            )
            if distance:
                held[distance // 2, :, cols] = mixed.astype(held.dtype)
            else:
                attended[:, cols] = (mixed * gate_ref[:, head : head + 1]).astype(jnp.bfloat16)
        if distance:
            send(distance)
    load.wait()
    width = out_ref.shape[1]

    def projected(target):
        cols = pl.ds(pl.multiple_of(target * width, 128), width)
        return jnp.dot(attended[...], w_out[:, cols], preferred_element_type=jnp.float32)

    def out_message(hop):
        return pltpu.make_async_remote_copy(
            src_ref=outgoing.at[hop],
            dst_ref=arrived.at[hop],
            send_sem=out_send.at[hop],
            recv_sem=out_recv.at[hop],
            device_id={"kv": (kv + hop) % kv_count},
        )

    for hop in range(1, kv_count):
        outgoing[hop] = projected((kv + hop) % kv_count).astype(jnp.bfloat16)
        copy = out_message(hop)
        copy.start()
        sent.append(copy)
    total = projected(kv)
    for hop in range(1, kv_count):
        out_message(hop).wait_recv()
        total = total + arrived[hop].astype(jnp.float32)
    out_ref[...] = (total + hidden_ref[...].astype(jnp.float32)).astype(jnp.bfloat16)
    for copy in sent:
        copy.wait_send()


def merge_parts(parts, lse, tree_mix, tree_lse, gate, w_out, hidden, count, kv_count):
    rows, width = parts.shape[1:]
    lanes = lse.shape[2]
    half = max(1, count // 2)
    vmem = pl.BlockSpec(memory_space=pltpu.VMEM)
    return pl.pallas_call(
        functools.partial(merge_kernel, count, kv_count),
        out_shape=jax.ShapeDtypeStruct(hidden.shape, jnp.bfloat16),
        in_specs=[vmem] * 5 + [pl.BlockSpec(memory_space=pltpu.HBM), vmem],
        out_specs=vmem,
        scratch_shapes=[
            pltpu.VMEM((count, rows, width), parts.dtype),
            pltpu.VMEM((count, 8, lanes), jnp.float32),
            pltpu.VMEM((count, 8, lanes), jnp.float32),
            pltpu.VMEM((half, rows, width), parts.dtype),
            pltpu.VMEM((half, 8, lanes), jnp.float32),
            pltpu.VMEM(w_out.shape, w_out.dtype),
            pltpu.VMEM((rows, width), jnp.bfloat16),
            pltpu.VMEM((kv_count,) + hidden.shape, jnp.bfloat16),
            pltpu.VMEM((kv_count,) + hidden.shape, jnp.bfloat16),
            pltpu.SemaphoreType.DMA((2, count)),
            pltpu.SemaphoreType.DMA((2, count)),
            pltpu.SemaphoreType.DMA,
            pltpu.SemaphoreType.DMA((kv_count,)),
            pltpu.SemaphoreType.DMA((kv_count,)),
        ],
        compiler_params=pltpu.CompilerParams(
            collective_id=1, has_side_effects=True, vmem_limit_bytes=48 * 2**20
        ),
        name="merge_parts",
    )(parts, lse, tree_mix, tree_lse, gate, w_out, hidden)


def pool_kernel(
    groups, per_kv, block, score_scale, first_ref, last_ref, member_ref, q_ref, k_ref, v_ref, o_ref, lse_ref
):
    requests, tree, width = q_ref.shape
    local_kv = k_ref.shape[1] // 128
    per_group = requests // groups
    base_two = score_scale / math.log(2.0)
    o_ref[...] = jnp.zeros_like(o_ref)
    lse_ref[...] = jnp.full(lse_ref.shape, NEGATIVE, jnp.float32)

    def attend(owners, first, last):
        count = len(owners) * per_kv * tree
        together = min(local_kv, 2 if len(owners) > 1 else 4)
        for base in range(0, local_kv, together):
            heads = range(base, base + together)
            rows = [
                [(owner, kv * per_kv + sub) for sub in range(per_kv) for owner in owners]
                for kv in heads
            ]
            queries = [
                jnp.concatenate(
                    [q_ref[owner, :, head * 128 : (head + 1) * 128] for owner, head in places], axis=0
                )
                for places in rows
            ]

            def visit(step, carry):
                start = pl.multiple_of(step * block, block)
                slots = start + lax.broadcasted_iota(jnp.int32, (1, block), 1)
                shown = (slots >= first) & (slots < last)
                out = []
                raw = [
                    lax.dot_general(
                        query,
                        k_ref[pl.ds(start, block), kv * 128 : (kv + 1) * 128],
                        (((1,), (1,)), ((), ())),
                        preferred_element_type=jnp.float32,
                    )
                    for kv, query in zip(heads, queries)
                ]
                for kv, scores, (run_max, run_sum, run_num) in zip(heads, raw, carry):
                    scores = jnp.where(shown, scores, NEGATIVE)
                    new_max = jnp.maximum(run_max, jnp.max(scores, axis=1, keepdims=True))
                    weights = jnp.exp2((scores - new_max) * base_two)
                    factor = jnp.exp2((run_max - new_max) * base_two)
                    run_sum = run_sum * factor + jnp.sum(weights, axis=1, keepdims=True)
                    run_num = run_num * factor + jnp.dot(
                        weights.astype(jnp.bfloat16),
                        v_ref[pl.ds(start, block), kv * 128 : (kv + 1) * 128],
                        preferred_element_type=jnp.float32,
                    )
                    out.append((new_max, run_sum, run_num))
                return tuple(out)

            empty = (
                jnp.full((count, 1), NEGATIVE, jnp.float32),
                jnp.zeros((count, 1), jnp.float32),
                jnp.zeros((count, 128), jnp.float32),
            )
            done = lax.fori_loop(
                first // block, (last + block - 1) // block, visit, (empty,) * together
            )
            for places, (run_max, run_sum, run_num) in zip(rows, done):
                mixed = (run_num / run_sum).astype(o_ref.dtype)
                lse = run_max * score_scale + jnp.log(run_sum)
                for place, (owner, head) in enumerate(places):
                    part = slice(place * tree, (place + 1) * tree)
                    o_ref[owner, :, head * 128 : (head + 1) * 128] = mixed[part]
                    lse_ref[owner, :, head : head + 1] = lse[part]

    def group_step(group, unused):
        first, last = first_ref[group], last_ref[group]

        @pl.when(last > first)
        def _():
            attend([member_ref[group * per_group + at] for at in range(per_group)], first, last)

        return unused

    def own_step(owner, unused):
        first, last = first_ref[groups + owner], last_ref[groups + owner]

        @pl.when(last > first)
        def _():
            attend([owner], first, last)

        return unused

    lax.fori_loop(0, groups, group_step, 0)
    lax.fori_loop(0, requests, own_step, 0)


def pool_attention(first, last, members, query, keys, values, groups, per_kv, score_scale):
    requests, tree, width = query.shape
    vmem = pl.BlockSpec(memory_space=pltpu.VMEM)
    smem = pl.BlockSpec(memory_space=pltpu.SMEM)
    return pl.pallas_call(
        functools.partial(pool_kernel, groups, per_kv, min(512, keys.shape[0]), score_scale),
        out_shape=(
            jax.ShapeDtypeStruct(query.shape, jnp.bfloat16),
            jax.ShapeDtypeStruct((requests, tree, 128), jnp.float32),
        ),
        in_specs=[smem, smem, smem, vmem, vmem, vmem],
        out_specs=(vmem, vmem),
        compiler_params=pltpu.CompilerParams(vmem_limit_bytes=48 * 2**20),
        name="pool_attention",
    )(first, last, members, query, keys, values)


def body(
    hidden,
    in_gain,
    w_query,
    key_projection_weight,
    value_projection_weight,
    w_gate,
    w_out,
    q_gain,
    k_gain,
    cache_keys,
    pooled_cache_values,
    prefix_len,
    own_len,
    request_group,
    parents,
    accepted_leaf,
):
    local_req, tree = parents.shape
    groups = prefix_len.shape[0]
    requests = own_len.shape[0]
    head_width = q_gain.shape[0]
    local_heads = w_gate.shape[1]
    local_kv = key_projection_weight.shape[1] // head_width
    per_kv = local_heads // local_kv
    local_tok = hidden.shape[0]
    pool_dev = cache_keys.shape[0]
    seq_index = lax.axis_index("seq")
    score_scale = 1.0 / math.sqrt(head_width)
    seq_count = requests // local_req
    kv_count = in_gain.shape[0] // hidden.shape[1]
    reach, depth_f = tree_paths(parents)
    all_reqs = jnp.arange(requests, dtype=jnp.int32)
    my_reqs = seq_index * local_req + jnp.arange(local_req, dtype=jnp.int32)
    my_pick = (my_reqs[:, None] == all_reqs[None, :]).astype(jnp.int32)
    my_group = jnp.sum(my_pick * request_group[None, :], axis=1)
    group_ids = jnp.arange(groups, dtype=jnp.int32)
    group_pick = (my_group[:, None] == group_ids[None, :]).astype(jnp.int32)
    context = jnp.sum(group_pick * prefix_len[None, :], axis=1) + jnp.sum(
        my_pick * own_len[None, :], axis=1
    )
    positions = (context[:, None].astype(jnp.float32) + depth_f).reshape(-1)
    cosine, sine = rope_tables(positions, head_width)
    seen = (reach[:, :, None, :] * jnp.eye(local_req, dtype=jnp.float32)[:, None, :, None]).reshape(
        local_tok, local_tok
    )
    gathered, key_new, value_new, tree_mix, tree_lse, gate = layer_front(
        hidden,
        in_gain,
        w_query,
        key_projection_weight,
        value_projection_weight,
        w_gate.T,
        q_gain,
        k_gain,
        cosine,
        sine,
        seen,
        seq_count,
        kv_count,
        score_scale,
    )
    lengths_all = jnp.concatenate([prefix_len, own_len])
    starts = jnp.cumsum(lengths_all) - lengths_all
    first = jnp.clip(starts - seq_index * pool_dev, 0, pool_dev)
    last = jnp.clip(starts + lengths_all - seq_index * pool_dev, 0, pool_dev)
    same = (request_group[:, None] == request_group[None, :]) & (all_reqs[None, :] < all_reqs[:, None])
    place = request_group * (requests // groups) + jnp.sum(same.astype(jnp.int32), axis=1)
    members = jnp.sum(
        (place[None, :] == all_reqs[:, None]).astype(jnp.int32) * all_reqs[None, :], axis=1
    )
    parts, part_lse = pool_attention(
        first,
        last,
        members,
        gathered.reshape(requests, tree, local_heads * head_width),
        cache_keys.reshape(pool_dev, local_kv * head_width),
        pooled_cache_values.reshape(pool_dev, local_kv * head_width),
        groups,
        per_kv,
        score_scale,
    )
    layer_out = merge_parts(
        parts.reshape(seq_count, local_tok, local_heads * head_width),
        part_lse.reshape(seq_count, local_tok, 128),
        tree_mix,
        tree_lse,
        gate,
        w_out,
        hidden,
        seq_count,
        kv_count,
    )
    tree_rows = jnp.concatenate(
        [
            key_new.reshape(local_req, tree, local_kv * head_width),
            value_new.reshape(local_req, tree, local_kv * head_width),
        ],
        axis=-1,
    )
    picked = accepted_rows(reach, depth_f, accepted_leaf, tree_rows)
    accepted_keys = picked[:, :, : local_kv * head_width]
    accepted_values = picked[:, :, local_kv * head_width :]
    return (layer_out, accepted_keys, accepted_values)


def solution(mesh):
    in_specs = (
        P("seq", "kv"),
        P(),
        P(None, "kv"),
        P(None, "kv"),
        P(None, "kv"),
        P(None, "kv"),
        P("kv", None),
        P(),
        P(),
        P("seq", "kv", None),
        P("seq", "kv", None),
        P(),
        P(),
        P(),
        P("seq", None),
        P("seq"),
    )
    out_specs = (P("seq", "kv"), P("seq", None, "kv"), P("seq", None, "kv"))
    return jax.shard_map(body, mesh=mesh, in_specs=in_specs, out_specs=out_specs, check_vma=False)
```

```python
import functools
import math

import jax
import jax.numpy as jnp
from jax import lax
from jax.experimental import pallas as pl
from jax.experimental.pallas import tpu as pltpu
from jax.sharding import PartitionSpec as P

EPSILON = 1e-06
ROPE_BASE = 1000000.0
NEGATIVE = -1e30


def rms_scale(values, scales):
    mean_square = jnp.mean(values * values, axis=-1, keepdims=True)
    return values * lax.rsqrt(mean_square + EPSILON) * scales


def rope_tables(positions, head_width):
    half_width = head_width // 2
    freqs = jnp.exp(
        jnp.arange(half_width, dtype=jnp.float32) * (-2.0 * math.log(ROPE_BASE) / head_width)
    )
    angles = positions[:, None] * freqs[None, :]
    cosine = jnp.cos(angles)
    sine = jnp.sin(angles)
    return (
        jnp.concatenate([cosine, cosine], axis=-1),
        jnp.concatenate([-sine, sine], axis=-1),
    )


def tree_paths(parents):
    width = parents.shape[-1]
    nodes = jnp.arange(width, dtype=jnp.int32)
    linked = (parents[:, :, None] == nodes[None, None, :]).astype(jnp.float32)
    identity_mat = jnp.eye(width, dtype=jnp.float32)
    reach = jnp.minimum(identity_mat[None] + linked * (1.0 - identity_mat[None]), 1.0)
    for squaring in range(max(1, (width - 1).bit_length())):
        reach = jnp.minimum(
            jnp.einsum("mij,mjk->mik", reach, reach, precision=lax.Precision.HIGHEST), 1.0
        )
    depth_f = jnp.sum(reach, axis=-1) - 1.0
    return (reach, depth_f)


def accepted_rows(reach, depth_f, leaves, tree_rows):
    width = reach.shape[-1]
    nodes = jnp.arange(width, dtype=jnp.int32)
    leaf_pick = (leaves[:, None] == nodes[None, :]).astype(jnp.float32)
    on_path = jnp.einsum("mi,mij->mj", leaf_pick, reach, precision=lax.Precision.HIGHEST)
    levels = (depth_f[:, None, :] == nodes.astype(jnp.float32)[None, :, None]).astype(jnp.float32)
    select = levels * on_path[:, None, :]
    return jnp.einsum(
        "mdj,mjc->mdc", select, tree_rows.astype(jnp.float32), precision=lax.Precision.HIGHEST
    ).astype(jnp.bfloat16)


def lowest(distance):
    return distance & -distance


def flip(index, distance):
    out = index
    bit = 1
    while bit <= distance:
        if distance & bit:
            out = out + bit * (1 - 2 * ((index // bit) % 2))
        bit *= 2
    return out


def one_bits(count):
    bits = []
    bit = 1
    while bit < count:
        bits.append(bit)
        bit *= 2
    return bits


def greet(me, count, kv, kv_count):
    barrier = pltpu.get_barrier_semaphore()
    bits = one_bits(count)
    for bit in bits:
        pl.semaphore_signal(barrier, inc=1, device_id={"seq": flip(me, bit)})
    for hop in range(1, kv_count):
        pl.semaphore_signal(barrier, inc=1, device_id={"kv": (kv + hop) % kv_count})
    pl.semaphore_wait(barrier, len(bits) + kv_count - 1)


def layer_kernel(
    count,
    kv_count,
    score_scale,
    hidden_ref,
    in_gain_ref,
    w_query_ref,
    w_key_ref,
    w_value_ref,
    w_gate_ref,
    q_gain_ref,
    k_gain_ref,
    cos_ref,
    sin_ref,
    seen_ref,
    all_ref,
    key_ref,
    value_ref,
    tree_ref,
    tree_lse_ref,
    gate_ref,
    wide,
    w_query,
    w_key,
    w_value,
    w_gate,
    in_gain,
    q_gain,
    k_gain,
    load_sem,
    wide_send,
    wide_recv,
    send_sem,
    recv_sem,
):
    me = lax.axis_index("seq")
    kv = lax.axis_index("kv")
    loads = [
        pltpu.make_async_copy(source, target, load_sem.at[which])
        for which, (source, target) in enumerate(
            [
                (hidden_ref, wide.at[kv]),
                (in_gain_ref, in_gain),
                (q_gain_ref, q_gain),
                (k_gain_ref, k_gain),
                (w_query_ref, w_query),
                (w_key_ref, w_key),
                (w_value_ref, w_value),
                (w_gate_ref, w_gate),
            ]
        )
    ]
    for load in loads:
        load.start()
    loads[0].wait()
    greet(me, count, kv, kv_count)

    def wide_message(hop, owner):
        return pltpu.make_async_remote_copy(
            src_ref=wide.at[owner],
            dst_ref=wide.at[owner],
            send_sem=wide_send.at[hop],
            recv_sem=wide_recv.at[hop],
            device_id={"kv": (kv + hop) % kv_count},
        )

    wide_sent = [wide_message(hop, kv) for hop in range(1, kv_count)]
    for copy in wide_sent:
        copy.start()
    for hop in range(1, kv_count):
        wide_message(hop, (kv + kv_count - hop) % kv_count).wait_recv()
    rows = jnp.concatenate([wide[at] for at in range(kv_count)], axis=1).astype(jnp.float32)
    for load in loads[1:4]:
        load.wait()
    normed = rms_scale(rows, in_gain[...]).astype(jnp.bfloat16)

    def rotated(values, gain):
        values = rms_scale(values, gain[...])
        return (values * cos_ref[...] + pltpu.roll(values, 64, 1) * sin_ref[...]).astype(jnp.bfloat16)

    loads[4].wait()
    query = jnp.dot(normed, w_query[...], preferred_element_type=jnp.float32)
    heads = query.shape[1] // 128
    queries = [rotated(query[:, h * 128 : (h + 1) * 128], q_gain) for h in range(heads)]
    for head in range(heads):
        all_ref[me, :, head * 128 : (head + 1) * 128] = queries[head]

    def message(distance, owner):
        return pltpu.make_async_remote_copy(
            src_ref=all_ref.at[owner],
            dst_ref=all_ref.at[owner],
            send_sem=send_sem.at[distance],
            recv_sem=recv_sem.at[distance],
            device_id={"seq": flip(me, lowest(distance))},
        )

    sent = []

    def hand_on(distance):
        owner = flip(me, distance)
        if distance:
            message(distance, owner).wait_recv()
        for bit in reversed(one_bits(lowest(distance) if distance else count)):
            copy = message(distance | bit, owner)
            copy.start()
            sent.append(copy)

    hand_on(0)
    local_kv = key_ref.shape[1] // 128
    per_kv = heads // local_kv
    tokens = hidden_ref.shape[0]

    def keys_work():
        loads[5].wait()
        key = jnp.dot(normed, w_key[...], preferred_element_type=jnp.float32)
        for at in range(local_kv):
            cols = slice(at * 128, (at + 1) * 128)
            key_ref[:, cols] = rotated(key[:, cols], k_gain)

    def values_work():
        loads[6].wait()
        loads[7].wait()
        value_ref[...] = jnp.dot(
            normed, w_value[...], preferred_element_type=jnp.float32
        ).astype(jnp.bfloat16)
        gate_ref[...] = jax.nn.sigmoid(
            lax.dot_general(
                normed, w_gate[...], (((1,), (1,)), ((), ())), preferred_element_type=jnp.float32
            )
        )
        tree_lse_ref[...] = jnp.zeros(tree_lse_ref.shape, jnp.float32)

    def tree_work(at):
        cols = slice(at * 128, (at + 1) * 128)
        stacked = jnp.concatenate(queries[at * per_kv : (at + 1) * per_kv], axis=0)
        scores = (
            lax.dot_general(
                stacked,
                key_ref[:, cols],
                (((1,), (1,)), ((), ())),
                preferred_element_type=jnp.float32,
            )
            * score_scale
        )
        seen = jnp.concatenate([seen_ref[...]] * per_kv, axis=0) > 0.5
        scores = jnp.where(seen, scores, NEGATIVE)
        top = jnp.max(scores, axis=1, keepdims=True)
        weights = jnp.where(seen, jnp.exp(scores - top), 0.0)
        total = jnp.sum(weights, axis=1, keepdims=True)
        mixed = (
            jnp.dot(
                weights.astype(jnp.bfloat16), value_ref[:, cols], preferred_element_type=jnp.float32
            )
            / total
        )
        lse = top + jnp.log(total)
        for sub in range(per_kv):
            head = at * per_kv + sub
            part = slice(sub * tokens, (sub + 1) * tokens)
            tree_ref[:, head * 128 : (head + 1) * 128] = mixed[part]
            tree_lse_ref[:, head : head + 1] = lse[part]

    work = [keys_work, values_work] + [functools.partial(tree_work, at) for at in range(local_kv)]
    order = sorted(range(2, count, 2), key=lambda d: (-lowest(d), d))
    for distance in order:
        if work:
            work.pop(0)()
        hand_on(distance)
    for rest in work:
        rest()
    for distance in range(1, count, 2):
        hand_on(distance)
    for copy in wide_sent + sent:
        copy.wait_send()


def layer_front(
    hidden, in_gain, w_query, w_key, w_value, w_gate, q_gain, k_gain, cosine, sine, seen, count, kv_count, score_scale
):
    tokens = hidden.shape[0]
    width = w_query.shape[1]
    vmem = pl.BlockSpec(memory_space=pltpu.VMEM)
    hbm = pl.BlockSpec(memory_space=pltpu.HBM)
    return pl.pallas_call(
        functools.partial(layer_kernel, count, kv_count, score_scale),
        out_shape=(
            jax.ShapeDtypeStruct((count, tokens, width), jnp.bfloat16),
            jax.ShapeDtypeStruct((tokens, w_key.shape[1]), jnp.bfloat16),
            jax.ShapeDtypeStruct((tokens, w_value.shape[1]), jnp.bfloat16),
            jax.ShapeDtypeStruct((tokens, width), jnp.float32),
            jax.ShapeDtypeStruct((tokens, 128), jnp.float32),
            jax.ShapeDtypeStruct((tokens, w_gate.shape[0]), jnp.float32),
        ),
        in_specs=[hbm] * 8 + [vmem] * 3,
        out_specs=(vmem,) * 6,
        scratch_shapes=[
            pltpu.VMEM((kv_count,) + hidden.shape, hidden.dtype),
            pltpu.VMEM(w_query.shape, w_query.dtype),
            pltpu.VMEM(w_key.shape, w_key.dtype),
            pltpu.VMEM(w_value.shape, w_value.dtype),
            pltpu.VMEM(w_gate.shape, w_gate.dtype),
            pltpu.VMEM((1, in_gain.shape[0]), jnp.float32),
            pltpu.VMEM((1, 128), jnp.float32),
            pltpu.VMEM((1, 128), jnp.float32),
            pltpu.SemaphoreType.DMA((8,)),
            pltpu.SemaphoreType.DMA((kv_count,)),
            pltpu.SemaphoreType.DMA((kv_count,)),
            pltpu.SemaphoreType.DMA((count,)),
            pltpu.SemaphoreType.DMA((count,)),
        ],
        compiler_params=pltpu.CompilerParams(
            collective_id=0, has_side_effects=True, vmem_limit_bytes=60 * 2**20
        ),
        name="layer_front",
    )(hidden, in_gain[None], w_query, w_key, w_value, w_gate, q_gain[None], k_gain[None], cosine, sine, seen)


def merge_kernel(
    count,
    kv_count,
    part_ref,
    lse_ref,
    tree_ref,
    tree_lse_ref,
    gate_ref,
    w_out_ref,
    hidden_ref,
    out_ref,
    got,
    got_lse,
    mine_lse,
    held,
    held_lse,
    w_out,
    attended,
    outgoing,
    arrived,
    send_sem,
    recv_sem,
    load_sem,
    out_send,
    out_recv,
):
    me = lax.axis_index("seq")
    kv = lax.axis_index("kv")
    heads = part_ref.shape[2] // 128
    load = pltpu.make_async_copy(w_out_ref, w_out, load_sem)
    load.start()
    rows = part_ref.shape[1]

    def across(level):
        turned = jnp.transpose(level)[:8]
        return jnp.concatenate([turned] * (128 // rows), axis=1)

    for distance in range(count):
        mine_lse[distance] = across(lse_ref[flip(me, distance)])
    greet(me, count, kv, kv_count)

    def messages(distance):
        owner = flip(me, distance)
        if distance % 2:
            sources = (part_ref.at[owner], mine_lse.at[distance])
        else:
            sources = (held.at[distance // 2], held_lse.at[distance // 2])
        return [
            pltpu.make_async_remote_copy(
                src_ref=source,
                dst_ref=target.at[distance],
                send_sem=send_sem.at[which, distance],
                recv_sem=recv_sem.at[which, distance],
                device_id={"seq": flip(me, lowest(distance))},
            )
            for which, (source, target) in enumerate(zip(sources, (got, got_lse)))
        ]

    sent = []

    def send(distance):
        for copy in messages(distance):
            copy.start()
            sent.append(copy)

    for distance in sorted(range(1, count, 2), reverse=True):
        send(distance)
    evens = sorted(range(2, count, 2), key=lambda d: (lowest(d), -d))
    for distance in evens + [0]:
        owner = flip(me, distance)
        incoming = [distance | bit for bit in one_bits(lowest(distance) if distance else count)]
        for message in incoming:
            for copy in messages(message):
                copy.wait_recv()
        levels = [mine_lse[distance]] + [got_lse[message] for message in incoming]
        if not distance:
            levels.append(across(tree_lse_ref[...]))
        top = functools.reduce(jnp.maximum, levels)
        shares = [jnp.exp(level - top) for level in levels]
        total = functools.reduce(jnp.add, shares)
        inverse = 1.0 / total
        shares = [jnp.transpose(share * inverse)[:rows] for share in shares]
        if distance:
            held_lse[distance // 2] = top + jnp.log(total)
        for head in range(heads):
            cols = slice(head * 128, (head + 1) * 128)
            pieces = [part_ref[owner, :, cols]] + [got[message, :, cols] for message in incoming]
            if not distance:
                pieces.append(tree_ref[:, cols])
            mixed = functools.reduce(
                jnp.add,
                [
                    piece.astype(jnp.float32) * share[:, head : head + 1]
                    for piece, share in zip(pieces, shares)
                ],
            )
            if distance:
                held[distance // 2, :, cols] = mixed.astype(held.dtype)
            else:
                attended[:, cols] = (mixed * gate_ref[:, head : head + 1]).astype(jnp.bfloat16)
        if distance:
            send(distance)
    load.wait()
    width = out_ref.shape[1]

    def projected(target):
        cols = pl.ds(pl.multiple_of(target * width, 128), width)
        return jnp.dot(attended[...], w_out[:, cols], preferred_element_type=jnp.float32)

    def out_message(hop):
        return pltpu.make_async_remote_copy(
            src_ref=outgoing.at[hop],
            dst_ref=arrived.at[hop],
            send_sem=out_send.at[hop],
            recv_sem=out_recv.at[hop],
            device_id={"kv": (kv + hop) % kv_count},
        )

    for hop in range(1, kv_count):
        outgoing[hop] = projected((kv + hop) % kv_count).astype(jnp.bfloat16)
        copy = out_message(hop)
        copy.start()
        sent.append(copy)
    total = projected(kv)
    for hop in range(1, kv_count):
        out_message(hop).wait_recv()
        total = total + arrived[hop].astype(jnp.float32)
    out_ref[...] = (total + hidden_ref[...].astype(jnp.float32)).astype(jnp.bfloat16)
    for copy in sent:
        copy.wait_send()


def merge_parts(parts, lse, tree_mix, tree_lse, gate, w_out, hidden, count, kv_count):
    rows, width = parts.shape[1:]
    lanes = lse.shape[2]
    half = max(1, count // 2)
    vmem = pl.BlockSpec(memory_space=pltpu.VMEM)
    return pl.pallas_call(
        functools.partial(merge_kernel, count, kv_count),
        out_shape=jax.ShapeDtypeStruct(hidden.shape, jnp.bfloat16),
        in_specs=[vmem] * 5 + [pl.BlockSpec(memory_space=pltpu.HBM), vmem],
        out_specs=vmem,
        scratch_shapes=[
            pltpu.VMEM((count, rows, width), parts.dtype),
            pltpu.VMEM((count, 8, lanes), jnp.float32),
            pltpu.VMEM((count, 8, lanes), jnp.float32),
            pltpu.VMEM((half, rows, width), parts.dtype),
            pltpu.VMEM((half, 8, lanes), jnp.float32),
            pltpu.VMEM(w_out.shape, w_out.dtype),
            pltpu.VMEM((rows, width), jnp.bfloat16),
            pltpu.VMEM((kv_count,) + hidden.shape, jnp.bfloat16),
            pltpu.VMEM((kv_count,) + hidden.shape, jnp.bfloat16),
            pltpu.SemaphoreType.DMA((2, count)),
            pltpu.SemaphoreType.DMA((2, count)),
            pltpu.SemaphoreType.DMA,
            pltpu.SemaphoreType.DMA((kv_count,)),
            pltpu.SemaphoreType.DMA((kv_count,)),
        ],
        compiler_params=pltpu.CompilerParams(
            collective_id=1, has_side_effects=True, vmem_limit_bytes=48 * 2**20
        ),
        name="merge_parts",
    )(parts, lse, tree_mix, tree_lse, gate, w_out, hidden)


def pool_kernel(
    groups,
    per_kv,
    block,
    score_scale,
    prefix_ref,
    own_ref,
    group_ref,
    q_ref,
    k_ref,
    v_ref,
    o_ref,
    lse_ref,
    first_ref,
    last_ref,
    member_ref,
    filled_ref,
):
    requests, tree, width = q_ref.shape
    local_kv = k_ref.shape[1] // 128
    per_group = requests // groups
    base_two = score_scale / math.log(2.0)
    pool_dev = k_ref.shape[0]
    offset = lax.axis_index("seq") * pool_dev

    def place(segment, start, length):
        stop = start + length
        first_ref[segment] = jnp.clip(start - offset, 0, pool_dev)
        last_ref[segment] = jnp.clip(stop - offset, 0, pool_dev)
        return stop

    def place_prefix(group, start):
        filled_ref[group] = 0
        return place(group, start, prefix_ref[group])

    def place_own(owner, start):
        group = group_ref[owner]
        at = filled_ref[group]
        member_ref[group * per_group + at] = owner
        filled_ref[group] = at + 1
        return place(groups + owner, start, own_ref[owner])

    lax.fori_loop(0, requests, place_own, lax.fori_loop(0, groups, place_prefix, 0))
    o_ref[...] = jnp.zeros_like(o_ref)
    lse_ref[...] = jnp.full(lse_ref.shape, NEGATIVE, jnp.float32)

    def attend(owners, first, last):
        count = len(owners) * per_kv * tree
        together = min(local_kv, 2 if len(owners) > 1 else 4)
        for base in range(0, local_kv, together):
            heads = range(base, base + together)
            rows = [
                [(owner, kv * per_kv + sub) for sub in range(per_kv) for owner in owners]
                for kv in heads
            ]
            queries = [
                jnp.concatenate(
                    [q_ref[owner, :, head * 128 : (head + 1) * 128] for owner, head in places], axis=0
                )
                for places in rows
            ]

            def visit(step, carry):
                start = pl.multiple_of(step * block, block)
                slots = start + lax.broadcasted_iota(jnp.int32, (1, block), 1)
                shown = (slots >= first) & (slots < last)
                out = []
                raw = [
                    lax.dot_general(
                        query,
                        k_ref[pl.ds(start, block), kv * 128 : (kv + 1) * 128],
                        (((1,), (1,)), ((), ())),
                        preferred_element_type=jnp.float32,
                    )
                    for kv, query in zip(heads, queries)
                ]
                for kv, scores, (run_max, run_sum, run_num) in zip(heads, raw, carry):
                    scores = jnp.where(shown, scores, NEGATIVE)
                    new_max = jnp.maximum(run_max, jnp.max(scores, axis=1, keepdims=True))
                    weights = jnp.exp2((scores - new_max) * base_two)
                    factor = jnp.exp2((run_max - new_max) * base_two)
                    run_sum = run_sum * factor + jnp.sum(weights, axis=1, keepdims=True)
                    run_num = run_num * factor + jnp.dot(
                        weights.astype(jnp.bfloat16),
                        v_ref[pl.ds(start, block), kv * 128 : (kv + 1) * 128],
                        preferred_element_type=jnp.float32,
                    )
                    out.append((new_max, run_sum, run_num))
                return tuple(out)

            empty = (
                jnp.full((count, 1), NEGATIVE, jnp.float32),
                jnp.zeros((count, 1), jnp.float32),
                jnp.zeros((count, 128), jnp.float32),
            )
            done = lax.fori_loop(
                first // block, (last + block - 1) // block, visit, (empty,) * together
            )
            for places, (run_max, run_sum, run_num) in zip(rows, done):
                mixed = (run_num / run_sum).astype(o_ref.dtype)
                lse = run_max * score_scale + jnp.log(run_sum)
                for place, (owner, head) in enumerate(places):
                    part = slice(place * tree, (place + 1) * tree)
                    o_ref[owner, :, head * 128 : (head + 1) * 128] = mixed[part]
                    lse_ref[owner, :, head : head + 1] = lse[part]

    def group_step(group, unused):
        first, last = first_ref[group], last_ref[group]

        @pl.when(last > first)
        def _():
            attend([member_ref[group * per_group + at] for at in range(per_group)], first, last)

        return unused

    def own_step(owner, unused):
        first, last = first_ref[groups + owner], last_ref[groups + owner]

        @pl.when(last > first)
        def _():
            attend([owner], first, last)

        return unused

    lax.fori_loop(0, groups, group_step, 0)
    lax.fori_loop(0, requests, own_step, 0)


def pool_attention(prefix_len, own_len, request_group, query, keys, values, groups, per_kv, score_scale):
    requests, tree, width = query.shape
    vmem = pl.BlockSpec(memory_space=pltpu.VMEM)
    smem = pl.BlockSpec(memory_space=pltpu.SMEM)
    return pl.pallas_call(
        functools.partial(pool_kernel, groups, per_kv, min(512, keys.shape[0]), score_scale),
        out_shape=(
            jax.ShapeDtypeStruct(query.shape, jnp.bfloat16),
            jax.ShapeDtypeStruct((requests, tree, 128), jnp.float32),
        ),
        in_specs=[smem, smem, smem, vmem, vmem, vmem],
        out_specs=(vmem, vmem),
        scratch_shapes=[
            pltpu.SMEM((groups + requests,), jnp.int32),
            pltpu.SMEM((groups + requests,), jnp.int32),
            pltpu.SMEM((requests,), jnp.int32),
            pltpu.SMEM((groups,), jnp.int32),
        ],
        compiler_params=pltpu.CompilerParams(vmem_limit_bytes=60 * 2**20),
        name="pool_attention",
    )(prefix_len, own_len, request_group, query, keys, values)


def body(
    hidden,
    in_gain,
    w_query,
    key_projection_weight,
    value_projection_weight,
    w_gate,
    w_out,
    q_gain,
    k_gain,
    cache_keys,
    pooled_cache_values,
    prefix_len,
    own_len,
    request_group,
    parents,
    accepted_leaf,
):
    local_req, tree = parents.shape
    groups = prefix_len.shape[0]
    requests = own_len.shape[0]
    head_width = q_gain.shape[0]
    local_heads = w_gate.shape[1]
    local_kv = key_projection_weight.shape[1] // head_width
    per_kv = local_heads // local_kv
    local_tok = hidden.shape[0]
    pool_dev = cache_keys.shape[0]
    seq_index = lax.axis_index("seq")
    score_scale = 1.0 / math.sqrt(head_width)
    seq_count = requests // local_req
    kv_count = in_gain.shape[0] // hidden.shape[1]
    reach, depth_f = tree_paths(parents)
    all_reqs = jnp.arange(requests, dtype=jnp.int32)
    my_reqs = seq_index * local_req + jnp.arange(local_req, dtype=jnp.int32)
    my_pick = (my_reqs[:, None] == all_reqs[None, :]).astype(jnp.int32)
    my_group = jnp.sum(my_pick * request_group[None, :], axis=1)
    group_ids = jnp.arange(groups, dtype=jnp.int32)
    group_pick = (my_group[:, None] == group_ids[None, :]).astype(jnp.int32)
    context = jnp.sum(group_pick * prefix_len[None, :], axis=1) + jnp.sum(
        my_pick * own_len[None, :], axis=1
    )
    positions = (context[:, None].astype(jnp.float32) + depth_f).reshape(-1)
    cosine, sine = rope_tables(positions, head_width)
    seen = (reach[:, :, None, :] * jnp.eye(local_req, dtype=jnp.float32)[:, None, :, None]).reshape(
        local_tok, local_tok
    )
    gathered, key_new, value_new, tree_mix, tree_lse, gate = layer_front(
        hidden,
        in_gain,
        w_query,
        key_projection_weight,
        value_projection_weight,
        w_gate.T,
        q_gain,
        k_gain,
        cosine,
        sine,
        seen,
        seq_count,
        kv_count,
        score_scale,
    )
    parts, part_lse = pool_attention(
        prefix_len,
        own_len,
        request_group,
        gathered.reshape(requests, tree, local_heads * head_width),
        cache_keys.reshape(pool_dev, local_kv * head_width),
        pooled_cache_values.reshape(pool_dev, local_kv * head_width),
        groups,
        per_kv,
        score_scale,
    )
    layer_out = merge_parts(
        parts.reshape(seq_count, local_tok, local_heads * head_width),
        part_lse.reshape(seq_count, local_tok, 128),
        tree_mix,
        tree_lse,
        gate,
        w_out,
        hidden,
        seq_count,
        kv_count,
    )
    tree_rows = jnp.concatenate(
        [
            key_new.reshape(local_req, tree, local_kv * head_width),
            value_new.reshape(local_req, tree, local_kv * head_width),
        ],
        axis=-1,
    )
    picked = accepted_rows(reach, depth_f, accepted_leaf, tree_rows)
    accepted_keys = picked[:, :, : local_kv * head_width]
    accepted_values = picked[:, :, local_kv * head_width :]
    return (layer_out, accepted_keys, accepted_values)


def solution(mesh):
    in_specs = (
        P("seq", "kv"),
        P(),
        P(None, "kv"),
        P(None, "kv"),
        P(None, "kv"),
        P(None, "kv"),
        P("kv", None),
        P(),
        P(),
        P("seq", "kv", None),
        P("seq", "kv", None),
        P(),
        P(),
        P(),
        P("seq", None),
        P("seq"),
    )
    out_specs = (P("seq", "kv"), P("seq", None, "kv"), P("seq", None, "kv"))
    return jax.shard_map(body, mesh=mesh, in_specs=in_specs, out_specs=out_specs, check_vma=False)
```

```python
import functools
import math

import jax
import jax.numpy as jnp
from jax import lax
from jax.experimental import pallas as pl
from jax.experimental.pallas import tpu as pltpu
from jax.sharding import PartitionSpec as P

EPSILON = 1e-06
ROPE_BASE = 1000000.0
NEGATIVE = -1e30


def rms_scale(values, scales):
    mean_square = jnp.mean(values * values, axis=-1, keepdims=True)
    return values * lax.rsqrt(mean_square + EPSILON) * scales


def rope_tables(positions, head_width):
    half_width = head_width // 2
    freqs = jnp.exp(
        jnp.arange(half_width, dtype=jnp.float32) * (-2.0 * math.log(ROPE_BASE) / head_width)
    )
    angles = positions[:, None] * freqs[None, :]
    cosine = jnp.cos(angles)
    sine = jnp.sin(angles)
    return (
        jnp.concatenate([cosine, cosine], axis=-1),
        jnp.concatenate([-sine, sine], axis=-1),
    )


def tree_paths(parents):
    width = parents.shape[-1]
    nodes = jnp.arange(width, dtype=jnp.int32)
    linked = (parents[:, :, None] == nodes[None, None, :]).astype(jnp.float32)
    identity_mat = jnp.eye(width, dtype=jnp.float32)
    reach = jnp.minimum(identity_mat[None] + linked * (1.0 - identity_mat[None]), 1.0)
    for squaring in range(max(1, (width - 1).bit_length())):
        reach = jnp.minimum(
            jnp.einsum("mij,mjk->mik", reach, reach, precision=lax.Precision.HIGHEST), 1.0
        )
    depth_f = jnp.sum(reach, axis=-1) - 1.0
    return (reach, depth_f)


def accepted_rows(reach, depth_f, leaves, tree_rows):
    width = reach.shape[-1]
    nodes = jnp.arange(width, dtype=jnp.int32)
    leaf_pick = (leaves[:, None] == nodes[None, :]).astype(jnp.float32)
    on_path = jnp.einsum("mi,mij->mj", leaf_pick, reach, precision=lax.Precision.HIGHEST)
    levels = (depth_f[:, None, :] == nodes.astype(jnp.float32)[None, :, None]).astype(jnp.float32)
    select = levels * on_path[:, None, :]
    return jnp.einsum(
        "mdj,mjc->mdc", select, tree_rows.astype(jnp.float32), precision=lax.Precision.HIGHEST
    ).astype(jnp.bfloat16)


def lowest(distance):
    return distance & -distance


def flip(index, distance):
    out = index
    bit = 1
    while bit <= distance:
        if distance & bit:
            out = out + bit * (1 - 2 * ((index // bit) % 2))
        bit *= 2
    return out


def one_bits(count):
    bits = []
    bit = 1
    while bit < count:
        bits.append(bit)
        bit *= 2
    return bits


def greet(me, count, kv, kv_count):
    barrier = pltpu.get_barrier_semaphore()
    bits = one_bits(count)
    for bit in bits:
        pl.semaphore_signal(barrier, inc=1, device_id={"seq": flip(me, bit)})
    for hop in range(1, kv_count):
        pl.semaphore_signal(barrier, inc=1, device_id={"kv": (kv + hop) % kv_count})
    pl.semaphore_wait(barrier, len(bits) + kv_count - 1)


def layer_kernel(
    count,
    kv_count,
    score_scale,
    hidden_ref,
    in_gain_ref,
    w_query_ref,
    w_key_ref,
    w_value_ref,
    w_gate_ref,
    q_gain_ref,
    k_gain_ref,
    cos_ref,
    sin_ref,
    seen_ref,
    all_ref,
    key_ref,
    value_ref,
    tree_ref,
    tree_lse_ref,
    gate_ref,
    wide,
    w_query,
    w_key,
    w_value,
    w_gate,
    in_gain,
    q_gain,
    k_gain,
    load_sem,
    wide_send,
    wide_recv,
    send_sem,
    recv_sem,
):
    me = lax.axis_index("seq")
    kv = lax.axis_index("kv")
    loads = [
        pltpu.make_async_copy(source, target, load_sem.at[which])
        for which, (source, target) in enumerate(
            [
                (hidden_ref, wide.at[kv]),
                (in_gain_ref, in_gain),
                (q_gain_ref, q_gain),
                (k_gain_ref, k_gain),
                (w_query_ref, w_query),
                (w_key_ref, w_key),
                (w_value_ref, w_value),
                (w_gate_ref, w_gate),
            ]
        )
    ]
    for load in loads:
        load.start()
    loads[0].wait()
    greet(me, count, kv, kv_count)

    def wide_message(hop, owner):
        return pltpu.make_async_remote_copy(
            src_ref=wide.at[owner],
            dst_ref=wide.at[owner],
            send_sem=wide_send.at[hop],
            recv_sem=wide_recv.at[hop],
            device_id={"kv": (kv + hop) % kv_count},
        )

    wide_sent = [wide_message(hop, kv) for hop in range(1, kv_count)]
    for copy in wide_sent:
        copy.start()
    for hop in range(1, kv_count):
        wide_message(hop, (kv + kv_count - hop) % kv_count).wait_recv()
    rows = jnp.concatenate([wide[at] for at in range(kv_count)], axis=1).astype(jnp.float32)
    for load in loads[1:4]:
        load.wait()
    normed = rms_scale(rows, in_gain[...]).astype(jnp.bfloat16)

    def rotated(values, gain):
        values = rms_scale(values, gain[...])
        return (values * cos_ref[...] + pltpu.roll(values, 64, 1) * sin_ref[...]).astype(jnp.bfloat16)

    loads[4].wait()
    query = jnp.dot(normed, w_query[...], preferred_element_type=jnp.float32)
    heads = query.shape[1] // 128
    queries = [rotated(query[:, h * 128 : (h + 1) * 128], q_gain) for h in range(heads)]
    for head in range(heads):
        all_ref[me, :, head * 128 : (head + 1) * 128] = queries[head]

    def message(distance, owner):
        return pltpu.make_async_remote_copy(
            src_ref=all_ref.at[owner],
            dst_ref=all_ref.at[owner],
            send_sem=send_sem.at[distance],
            recv_sem=recv_sem.at[distance],
            device_id={"seq": flip(me, lowest(distance))},
        )

    sent = []

    def hand_on(distance):
        owner = flip(me, distance)
        if distance:
            message(distance, owner).wait_recv()
        for bit in reversed(one_bits(lowest(distance) if distance else count)):
            copy = message(distance | bit, owner)
            copy.start()
            sent.append(copy)

    hand_on(0)
    local_kv = key_ref.shape[1] // 128
    per_kv = heads // local_kv
    tokens = hidden_ref.shape[0]

    def keys_work():
        loads[5].wait()
        key = jnp.dot(normed, w_key[...], preferred_element_type=jnp.float32)
        for at in range(local_kv):
            cols = slice(at * 128, (at + 1) * 128)
            key_ref[:, cols] = rotated(key[:, cols], k_gain)

    def values_work():
        loads[6].wait()
        loads[7].wait()
        value_ref[...] = jnp.dot(
            normed, w_value[...], preferred_element_type=jnp.float32
        ).astype(jnp.bfloat16)
        gate_ref[...] = jax.nn.sigmoid(
            lax.dot_general(
                normed, w_gate[...], (((1,), (1,)), ((), ())), preferred_element_type=jnp.float32
            )
        )
        tree_lse_ref[...] = jnp.zeros(tree_lse_ref.shape, jnp.float32)

    def tree_work(at):
        cols = slice(at * 128, (at + 1) * 128)
        stacked = jnp.concatenate(queries[at * per_kv : (at + 1) * per_kv], axis=0)
        scores = (
            lax.dot_general(
                stacked,
                key_ref[:, cols],
                (((1,), (1,)), ((), ())),
                preferred_element_type=jnp.float32,
            )
            * score_scale
        )
        seen = jnp.concatenate([seen_ref[...]] * per_kv, axis=0) > 0.5
        scores = jnp.where(seen, scores, NEGATIVE)
        top = jnp.max(scores, axis=1, keepdims=True)
        weights = jnp.where(seen, jnp.exp(scores - top), 0.0)
        total = jnp.sum(weights, axis=1, keepdims=True)
        mixed = (
            jnp.dot(
                weights.astype(jnp.bfloat16), value_ref[:, cols], preferred_element_type=jnp.float32
            )
            / total
        )
        lse = top + jnp.log(total)
        for sub in range(per_kv):
            head = at * per_kv + sub
            part = slice(sub * tokens, (sub + 1) * tokens)
            tree_ref[:, head * 128 : (head + 1) * 128] = mixed[part]
            tree_lse_ref[:, head : head + 1] = lse[part]

    work = [keys_work, values_work] + [functools.partial(tree_work, at) for at in range(local_kv)]
    order = sorted(range(2, count, 2), key=lambda d: (-lowest(d), d))
    for distance in order:
        if work:
            work.pop(0)()
        hand_on(distance)
    for rest in work:
        rest()
    for distance in range(1, count, 2):
        hand_on(distance)
    for copy in wide_sent + sent:
        copy.wait_send()


def layer_front(
    hidden, in_gain, w_query, w_key, w_value, w_gate, q_gain, k_gain, cosine, sine, seen, count, kv_count, score_scale
):
    tokens = hidden.shape[0]
    width = w_query.shape[1]
    vmem = pl.BlockSpec(memory_space=pltpu.VMEM)
    hbm = pl.BlockSpec(memory_space=pltpu.HBM)
    return pl.pallas_call(
        functools.partial(layer_kernel, count, kv_count, score_scale),
        out_shape=(
            jax.ShapeDtypeStruct((count, tokens, width), jnp.bfloat16),
            jax.ShapeDtypeStruct((tokens, w_key.shape[1]), jnp.bfloat16),
            jax.ShapeDtypeStruct((tokens, w_value.shape[1]), jnp.bfloat16),
            jax.ShapeDtypeStruct((tokens, width), jnp.float32),
            jax.ShapeDtypeStruct((tokens, 128), jnp.float32),
            jax.ShapeDtypeStruct((tokens, w_gate.shape[0]), jnp.float32),
        ),
        in_specs=[hbm] * 8 + [vmem] * 3,
        out_specs=(vmem,) * 6,
        scratch_shapes=[
            pltpu.VMEM((kv_count,) + hidden.shape, hidden.dtype),
            pltpu.VMEM(w_query.shape, w_query.dtype),
            pltpu.VMEM(w_key.shape, w_key.dtype),
            pltpu.VMEM(w_value.shape, w_value.dtype),
            pltpu.VMEM(w_gate.shape, w_gate.dtype),
            pltpu.VMEM((1, in_gain.shape[0]), jnp.float32),
            pltpu.VMEM((1, 128), jnp.float32),
            pltpu.VMEM((1, 128), jnp.float32),
            pltpu.SemaphoreType.DMA((8,)),
            pltpu.SemaphoreType.DMA((kv_count,)),
            pltpu.SemaphoreType.DMA((kv_count,)),
            pltpu.SemaphoreType.DMA((count,)),
            pltpu.SemaphoreType.DMA((count,)),
        ],
        compiler_params=pltpu.CompilerParams(
            collective_id=0, has_side_effects=True, vmem_limit_bytes=60 * 2**20
        ),
        name="layer_front",
    )(hidden, in_gain[None], w_query, w_key, w_value, w_gate, q_gain[None], k_gain[None], cosine, sine, seen)


def merge_kernel(
    count,
    kv_count,
    part_ref,
    lse_ref,
    tree_ref,
    tree_lse_ref,
    gate_ref,
    w_out_ref,
    hidden_ref,
    out_ref,
    got,
    got_lse,
    mine_lse,
    held,
    held_lse,
    w_out,
    attended,
    outgoing,
    arrived,
    send_sem,
    recv_sem,
    load_sem,
    out_send,
    out_recv,
):
    me = lax.axis_index("seq")
    kv = lax.axis_index("kv")
    heads = part_ref.shape[2] // 128
    load = pltpu.make_async_copy(w_out_ref, w_out, load_sem)
    load.start()
    rows = part_ref.shape[1]

    def across(level):
        turned = jnp.transpose(level)[:8]
        return jnp.concatenate([turned] * (128 // rows), axis=1)

    for distance in range(count):
        mine_lse[distance] = across(lse_ref[flip(me, distance)])
    greet(me, count, kv, kv_count)

    def messages(distance):
        owner = flip(me, distance)
        if distance % 2:
            sources = (part_ref.at[owner], mine_lse.at[distance])
        else:
            sources = (held.at[distance // 2], held_lse.at[distance // 2])
        return [
            pltpu.make_async_remote_copy(
                src_ref=source,
                dst_ref=target.at[distance],
                send_sem=send_sem.at[which, distance],
                recv_sem=recv_sem.at[which, distance],
                device_id={"seq": flip(me, lowest(distance))},
            )
            for which, (source, target) in enumerate(zip(sources, (got, got_lse)))
        ]

    sent = []

    def send(distance):
        for copy in messages(distance):
            copy.start()
            sent.append(copy)

    for distance in sorted(range(1, count, 2), reverse=True):
        send(distance)
    evens = sorted(range(2, count, 2), key=lambda d: (lowest(d), -d))
    for distance in evens + [0]:
        owner = flip(me, distance)
        incoming = [distance | bit for bit in one_bits(lowest(distance) if distance else count)]
        for message in incoming:
            for copy in messages(message):
                copy.wait_recv()
        levels = [mine_lse[distance]] + [got_lse[message] for message in incoming]
        if not distance:
            levels.append(across(tree_lse_ref[...]))
        top = functools.reduce(jnp.maximum, levels)
        shares = [jnp.exp(level - top) for level in levels]
        total = functools.reduce(jnp.add, shares)
        inverse = 1.0 / total
        shares = [jnp.transpose(share * inverse)[:rows] for share in shares]
        if distance:
            held_lse[distance // 2] = top + jnp.log(total)
        for head in range(heads):
            cols = slice(head * 128, (head + 1) * 128)
            pieces = [part_ref[owner, :, cols]] + [got[message, :, cols] for message in incoming]
            if not distance:
                pieces.append(tree_ref[:, cols])
            mixed = functools.reduce(
                jnp.add,
                [
                    piece.astype(jnp.float32) * share[:, head : head + 1]
                    for piece, share in zip(pieces, shares)
                ],
            )
            if distance:
                held[distance // 2, :, cols] = mixed.astype(held.dtype)
            else:
                attended[:, cols] = (mixed * gate_ref[:, head : head + 1]).astype(jnp.bfloat16)
        if distance:
            send(distance)
    load.wait()
    width = out_ref.shape[1]

    def projected(target):
        cols = pl.ds(pl.multiple_of(target * width, 128), width)
        return jnp.dot(attended[...], w_out[:, cols], preferred_element_type=jnp.float32)

    def out_message(hop):
        return pltpu.make_async_remote_copy(
            src_ref=outgoing.at[hop],
            dst_ref=arrived.at[hop],
            send_sem=out_send.at[hop],
            recv_sem=out_recv.at[hop],
            device_id={"kv": (kv + hop) % kv_count},
        )

    for hop in range(1, kv_count):
        outgoing[hop] = projected((kv + hop) % kv_count).astype(jnp.bfloat16)
        copy = out_message(hop)
        copy.start()
        sent.append(copy)
    total = projected(kv)
    for hop in range(1, kv_count):
        out_message(hop).wait_recv()
        total = total + arrived[hop].astype(jnp.float32)
    out_ref[...] = (total + hidden_ref[...].astype(jnp.float32)).astype(jnp.bfloat16)
    for copy in sent:
        copy.wait_send()


def merge_parts(parts, lse, tree_mix, tree_lse, gate, w_out, hidden, count, kv_count):
    rows, width = parts.shape[1:]
    lanes = lse.shape[2]
    half = max(1, count // 2)
    vmem = pl.BlockSpec(memory_space=pltpu.VMEM)
    return pl.pallas_call(
        functools.partial(merge_kernel, count, kv_count),
        out_shape=jax.ShapeDtypeStruct(hidden.shape, jnp.bfloat16),
        in_specs=[vmem] * 5 + [pl.BlockSpec(memory_space=pltpu.HBM), vmem],
        out_specs=vmem,
        scratch_shapes=[
            pltpu.VMEM((count, rows, width), parts.dtype),
            pltpu.VMEM((count, 8, lanes), jnp.float32),
            pltpu.VMEM((count, 8, lanes), jnp.float32),
            pltpu.VMEM((half, rows, width), parts.dtype),
            pltpu.VMEM((half, 8, lanes), jnp.float32),
            pltpu.VMEM(w_out.shape, w_out.dtype),
            pltpu.VMEM((rows, width), jnp.bfloat16),
            pltpu.VMEM((kv_count,) + hidden.shape, jnp.bfloat16),
            pltpu.VMEM((kv_count,) + hidden.shape, jnp.bfloat16),
            pltpu.SemaphoreType.DMA((2, count)),
            pltpu.SemaphoreType.DMA((2, count)),
            pltpu.SemaphoreType.DMA,
            pltpu.SemaphoreType.DMA((kv_count,)),
            pltpu.SemaphoreType.DMA((kv_count,)),
        ],
        compiler_params=pltpu.CompilerParams(
            collective_id=1, has_side_effects=True, vmem_limit_bytes=48 * 2**20
        ),
        name="merge_parts",
    )(parts, lse, tree_mix, tree_lse, gate, w_out, hidden)


def pool_kernel(
    groups,
    per_kv,
    block,
    score_scale,
    facts_ref,
    q_ref,
    k_ref,
    v_ref,
    o_ref,
    lse_ref,
    first_ref,
    last_ref,
    member_ref,
    filled_ref,
):
    requests, tree, width = q_ref.shape
    local_kv = k_ref.shape[1] // 128
    per_group = requests // groups
    base_two = score_scale / math.log(2.0)
    pool_dev = k_ref.shape[0]
    offset = lax.axis_index("seq") * pool_dev

    def place(segment, start, length):
        stop = start + length
        first_ref[segment] = jnp.clip(start - offset, 0, pool_dev)
        last_ref[segment] = jnp.clip(stop - offset, 0, pool_dev)
        return stop

    def place_prefix(group, start):
        filled_ref[group] = 0
        return place(group, start, facts_ref[group])

    def place_own(owner, start):
        group = facts_ref[groups + requests + owner]
        at = filled_ref[group]
        member_ref[group * per_group + at] = owner
        filled_ref[group] = at + 1
        return place(groups + owner, start, facts_ref[groups + owner])

    lax.fori_loop(0, requests, place_own, lax.fori_loop(0, groups, place_prefix, 0))
    o_ref[...] = jnp.zeros_like(o_ref)
    lse_ref[...] = jnp.full(lse_ref.shape, NEGATIVE, jnp.float32)

    def attend(owners, first, last):
        count = len(owners) * per_kv * tree
        together = min(local_kv, 2 if len(owners) > 1 else 4)
        for base in range(0, local_kv, together):
            heads = range(base, base + together)
            rows = [
                [(owner, kv * per_kv + sub) for sub in range(per_kv) for owner in owners]
                for kv in heads
            ]
            queries = [
                jnp.concatenate(
                    [q_ref[owner, :, head * 128 : (head + 1) * 128] for owner, head in places], axis=0
                )
                for places in rows
            ]

            def visit(step, carry):
                start = pl.multiple_of(step * block, block)
                slots = start + lax.broadcasted_iota(jnp.int32, (1, block), 1)
                shown = (slots >= first) & (slots < last)
                out = []
                raw = [
                    lax.dot_general(
                        query,
                        k_ref[pl.ds(start, block), kv * 128 : (kv + 1) * 128],
                        (((1,), (1,)), ((), ())),
                        preferred_element_type=jnp.float32,
                    )
                    for kv, query in zip(heads, queries)
                ]
                for kv, scores, (run_max, run_sum, run_num) in zip(heads, raw, carry):
                    scores = jnp.where(shown, scores, NEGATIVE)
                    new_max = jnp.maximum(run_max, jnp.max(scores, axis=1, keepdims=True))
                    weights = jnp.exp2((scores - new_max) * base_two)
                    factor = jnp.exp2((run_max - new_max) * base_two)
                    run_sum = run_sum * factor + jnp.sum(weights, axis=1, keepdims=True)
                    run_num = run_num * factor + jnp.dot(
                        weights.astype(jnp.bfloat16),
                        v_ref[pl.ds(start, block), kv * 128 : (kv + 1) * 128],
                        preferred_element_type=jnp.float32,
                    )
                    out.append((new_max, run_sum, run_num))
                return tuple(out)

            empty = (
                jnp.full((count, 1), NEGATIVE, jnp.float32),
                jnp.zeros((count, 1), jnp.float32),
                jnp.zeros((count, 128), jnp.float32),
            )
            done = lax.fori_loop(
                first // block, (last + block - 1) // block, visit, (empty,) * together
            )
            for places, (run_max, run_sum, run_num) in zip(rows, done):
                mixed = (run_num / run_sum).astype(o_ref.dtype)
                lse = run_max * score_scale + jnp.log(run_sum)
                for place, (owner, head) in enumerate(places):
                    part = slice(place * tree, (place + 1) * tree)
                    o_ref[owner, :, head * 128 : (head + 1) * 128] = mixed[part]
                    lse_ref[owner, :, head : head + 1] = lse[part]

    def group_step(group, unused):
        first, last = first_ref[group], last_ref[group]

        @pl.when(last > first)
        def _():
            attend([member_ref[group * per_group + at] for at in range(per_group)], first, last)

        return unused

    def own_step(owner, unused):
        first, last = first_ref[groups + owner], last_ref[groups + owner]

        @pl.when(last > first)
        def _():
            attend([owner], first, last)

        return unused

    lax.fori_loop(0, groups, group_step, 0)
    lax.fori_loop(0, requests, own_step, 0)


def pool_attention(facts, query, keys, values, groups, per_kv, score_scale):
    requests, tree, width = query.shape
    vmem = pl.BlockSpec(memory_space=pltpu.VMEM)
    smem = pl.BlockSpec(memory_space=pltpu.SMEM)
    return pl.pallas_call(
        functools.partial(pool_kernel, groups, per_kv, min(512, keys.shape[0]), score_scale),
        out_shape=(
            jax.ShapeDtypeStruct(query.shape, jnp.bfloat16),
            jax.ShapeDtypeStruct((requests, tree, 128), jnp.float32),
        ),
        in_specs=[smem, vmem, vmem, vmem],
        out_specs=(vmem, vmem),
        scratch_shapes=[
            pltpu.SMEM((groups + requests,), jnp.int32),
            pltpu.SMEM((groups + requests,), jnp.int32),
            pltpu.SMEM((requests,), jnp.int32),
            pltpu.SMEM((groups,), jnp.int32),
        ],
        compiler_params=pltpu.CompilerParams(vmem_limit_bytes=48 * 2**20),
        name="pool_attention",
    )(facts, query, keys, values)


def body(
    hidden,
    in_gain,
    w_query,
    key_projection_weight,
    value_projection_weight,
    w_gate,
    w_out,
    q_gain,
    k_gain,
    cache_keys,
    pooled_cache_values,
    prefix_len,
    own_len,
    request_group,
    parents,
    accepted_leaf,
):
    local_req, tree = parents.shape
    groups = prefix_len.shape[0]
    requests = own_len.shape[0]
    head_width = q_gain.shape[0]
    local_heads = w_gate.shape[1]
    local_kv = key_projection_weight.shape[1] // head_width
    per_kv = local_heads // local_kv
    local_tok = hidden.shape[0]
    pool_dev = cache_keys.shape[0]
    seq_index = lax.axis_index("seq")
    score_scale = 1.0 / math.sqrt(head_width)
    seq_count = requests // local_req
    kv_count = in_gain.shape[0] // hidden.shape[1]
    reach, depth_f = tree_paths(parents)
    all_reqs = jnp.arange(requests, dtype=jnp.int32)
    my_reqs = seq_index * local_req + jnp.arange(local_req, dtype=jnp.int32)
    my_pick = (my_reqs[:, None] == all_reqs[None, :]).astype(jnp.int32)
    my_group = jnp.sum(my_pick * request_group[None, :], axis=1)
    group_ids = jnp.arange(groups, dtype=jnp.int32)
    group_pick = (my_group[:, None] == group_ids[None, :]).astype(jnp.int32)
    context = jnp.sum(group_pick * prefix_len[None, :], axis=1) + jnp.sum(
        my_pick * own_len[None, :], axis=1
    )
    positions = (context[:, None].astype(jnp.float32) + depth_f).reshape(-1)
    cosine, sine = rope_tables(positions, head_width)
    seen = (reach[:, :, None, :] * jnp.eye(local_req, dtype=jnp.float32)[:, None, :, None]).reshape(
        local_tok, local_tok
    )
    gathered, key_new, value_new, tree_mix, tree_lse, gate = layer_front(
        hidden,
        in_gain,
        w_query,
        key_projection_weight,
        value_projection_weight,
        w_gate.T,
        q_gain,
        k_gain,
        cosine,
        sine,
        seen,
        seq_count,
        kv_count,
        score_scale,
    )
    parts, part_lse = pool_attention(
        jnp.concatenate([prefix_len, own_len, request_group]),
        gathered.reshape(requests, tree, local_heads * head_width),
        cache_keys.reshape(pool_dev, local_kv * head_width),
        pooled_cache_values.reshape(pool_dev, local_kv * head_width),
        groups,
        per_kv,
        score_scale,
    )
    layer_out = merge_parts(
        parts.reshape(seq_count, local_tok, local_heads * head_width),
        part_lse.reshape(seq_count, local_tok, 128),
        tree_mix,
        tree_lse,
        gate,
        w_out,
        hidden,
        seq_count,
        kv_count,
    )
    tree_rows = jnp.concatenate(
        [
            key_new.reshape(local_req, tree, local_kv * head_width),
            value_new.reshape(local_req, tree, local_kv * head_width),
        ],
        axis=-1,
    )
    picked = accepted_rows(reach, depth_f, accepted_leaf, tree_rows)
    accepted_keys = picked[:, :, : local_kv * head_width]
    accepted_values = picked[:, :, local_kv * head_width :]
    return (layer_out, accepted_keys, accepted_values)


def solution(mesh):
    in_specs = (
        P("seq", "kv"),
        P(),
        P(None, "kv"),
        P(None, "kv"),
        P(None, "kv"),
        P(None, "kv"),
        P("kv", None),
        P(),
        P(),
        P("seq", "kv", None),
        P("seq", "kv", None),
        P(),
        P(),
        P(),
        P("seq", None),
        P("seq"),
    )
    out_specs = (P("seq", "kv"), P("seq", None, "kv"), P("seq", None, "kv"))
    return jax.shard_map(body, mesh=mesh, in_specs=in_specs, out_specs=out_specs, check_vma=False)
```

```python
import functools
import math

import jax
import jax.numpy as jnp
from jax import lax
from jax.experimental import pallas as pl
from jax.experimental.pallas import tpu as pltpu
from jax.sharding import PartitionSpec as P

EPSILON = 1e-06
ROPE_BASE = 1000000.0
NEGATIVE = -1e30


def rms_scale(values, scales):
    mean_square = jnp.mean(values * values, axis=-1, keepdims=True)
    return values * lax.rsqrt(mean_square + EPSILON) * scales


def rope_tables(positions, head_width):
    half_width = head_width // 2
    freqs = jnp.exp(
        jnp.arange(half_width, dtype=jnp.float32) * (-2.0 * math.log(ROPE_BASE) / head_width)
    )
    angles = positions[:, None] * freqs[None, :]
    cosine = jnp.cos(angles)
    sine = jnp.sin(angles)
    return (
        jnp.concatenate([cosine, cosine], axis=-1),
        jnp.concatenate([-sine, sine], axis=-1),
    )


def tree_paths(parents):
    width = parents.shape[-1]
    nodes = jnp.arange(width, dtype=jnp.int32)
    linked = (parents[:, :, None] == nodes[None, None, :]).astype(jnp.float32)
    identity_mat = jnp.eye(width, dtype=jnp.float32)
    reach = jnp.minimum(identity_mat[None] + linked * (1.0 - identity_mat[None]), 1.0)
    for squaring in range(max(1, (width - 1).bit_length())):
        reach = jnp.minimum(
            jnp.einsum("mij,mjk->mik", reach, reach, precision=lax.Precision.HIGHEST), 1.0
        )
    depth_f = jnp.sum(reach, axis=-1) - 1.0
    return (reach, depth_f)


def accepted_rows(reach, depth_f, leaves, tree_rows):
    width = reach.shape[-1]
    nodes = jnp.arange(width, dtype=jnp.int32)
    leaf_pick = (leaves[:, None] == nodes[None, :]).astype(jnp.float32)
    on_path = jnp.einsum("mi,mij->mj", leaf_pick, reach, precision=lax.Precision.HIGHEST)
    levels = (depth_f[:, None, :] == nodes.astype(jnp.float32)[None, :, None]).astype(jnp.float32)
    select = levels * on_path[:, None, :]
    return jnp.einsum(
        "mdj,mjc->mdc", select, tree_rows.astype(jnp.float32), precision=lax.Precision.HIGHEST
    ).astype(jnp.bfloat16)


def lowest(distance):
    return distance & -distance


def flip(index, distance):
    out = index
    bit = 1
    while bit <= distance:
        if distance & bit:
            out = out + bit * (1 - 2 * ((index // bit) % 2))
        bit *= 2
    return out


def one_bits(count):
    bits = []
    bit = 1
    while bit < count:
        bits.append(bit)
        bit *= 2
    return bits


def greet(me, count, kv, kv_count):
    barrier = pltpu.get_barrier_semaphore()
    bits = one_bits(count)
    for bit in bits:
        pl.semaphore_signal(barrier, inc=1, device_id={"seq": flip(me, bit)})
    for hop in range(1, kv_count):
        pl.semaphore_signal(barrier, inc=1, device_id={"kv": (kv + hop) % kv_count})
    pl.semaphore_wait(barrier, len(bits) + kv_count - 1)


def layer_kernel(
    count,
    kv_count,
    score_scale,
    hidden_ref,
    in_gain_ref,
    w_query_ref,
    w_key_ref,
    w_value_ref,
    w_gate_ref,
    q_gain_ref,
    k_gain_ref,
    cos_ref,
    sin_ref,
    seen_ref,
    all_ref,
    key_ref,
    value_ref,
    tree_ref,
    tree_lse_ref,
    gate_ref,
    wide,
    w_query,
    w_key,
    w_value,
    w_gate,
    in_gain,
    q_gain,
    k_gain,
    load_sem,
    wide_send,
    wide_recv,
    send_sem,
    recv_sem,
):
    me = lax.axis_index("seq")
    kv = lax.axis_index("kv")
    loads = [
        pltpu.make_async_copy(source, target, load_sem.at[which])
        for which, (source, target) in enumerate(
            [
                (hidden_ref, wide.at[kv]),
                (in_gain_ref, in_gain),
                (q_gain_ref, q_gain),
                (k_gain_ref, k_gain),
                (w_query_ref, w_query),
                (w_key_ref, w_key),
                (w_value_ref, w_value),
                (w_gate_ref, w_gate),
            ]
        )
    ]
    for load in loads:
        load.start()
    loads[0].wait()
    greet(me, count, kv, kv_count)

    def wide_message(hop, owner):
        return pltpu.make_async_remote_copy(
            src_ref=wide.at[owner],
            dst_ref=wide.at[owner],
            send_sem=wide_send.at[hop],
            recv_sem=wide_recv.at[hop],
            device_id={"kv": (kv + hop) % kv_count},
        )

    wide_sent = [wide_message(hop, kv) for hop in range(1, kv_count)]
    for copy in wide_sent:
        copy.start()
    for hop in range(1, kv_count):
        wide_message(hop, (kv + kv_count - hop) % kv_count).wait_recv()
    rows = jnp.concatenate([wide[at] for at in range(kv_count)], axis=1).astype(jnp.float32)
    for load in loads[1:4]:
        load.wait()
    normed = rms_scale(rows, in_gain[...]).astype(jnp.bfloat16)

    def rotated(values, gain):
        values = rms_scale(values, gain[...])
        return (values * cos_ref[...] + pltpu.roll(values, 64, 1) * sin_ref[...]).astype(jnp.bfloat16)

    loads[4].wait()
    query = jnp.dot(normed, w_query[...], preferred_element_type=jnp.float32)
    heads = query.shape[1] // 128
    queries = [rotated(query[:, h * 128 : (h + 1) * 128], q_gain) for h in range(heads)]
    for head in range(heads):
        all_ref[me, :, head * 128 : (head + 1) * 128] = queries[head]

    def message(distance, owner):
        return pltpu.make_async_remote_copy(
            src_ref=all_ref.at[owner],
            dst_ref=all_ref.at[owner],
            send_sem=send_sem.at[distance],
            recv_sem=recv_sem.at[distance],
            device_id={"seq": flip(me, lowest(distance))},
        )

    sent = []

    def hand_on(distance):
        owner = flip(me, distance)
        if distance:
            message(distance, owner).wait_recv()
        for bit in reversed(one_bits(lowest(distance) if distance else count)):
            copy = message(distance | bit, owner)
            copy.start()
            sent.append(copy)

    hand_on(0)
    local_kv = key_ref.shape[1] // 128
    per_kv = heads // local_kv
    tokens = hidden_ref.shape[0]

    def keys_work():
        loads[5].wait()
        key = jnp.dot(normed, w_key[...], preferred_element_type=jnp.float32)
        for at in range(local_kv):
            cols = slice(at * 128, (at + 1) * 128)
            key_ref[:, cols] = rotated(key[:, cols], k_gain)

    def values_work():
        loads[6].wait()
        loads[7].wait()
        value_ref[...] = jnp.dot(
            normed, w_value[...], preferred_element_type=jnp.float32
        ).astype(jnp.bfloat16)
        gate_ref[...] = jax.nn.sigmoid(
            lax.dot_general(
                normed, w_gate[...], (((1,), (1,)), ((), ())), preferred_element_type=jnp.float32
            )
        )
        tree_lse_ref[...] = jnp.zeros(tree_lse_ref.shape, jnp.float32)

    def tree_work(at):
        cols = slice(at * 128, (at + 1) * 128)
        stacked = jnp.concatenate(queries[at * per_kv : (at + 1) * per_kv], axis=0)
        scores = (
            lax.dot_general(
                stacked,
                key_ref[:, cols],
                (((1,), (1,)), ((), ())),
                preferred_element_type=jnp.float32,
            )
            * score_scale
        )
        seen = jnp.concatenate([seen_ref[...]] * per_kv, axis=0) > 0.5
        scores = jnp.where(seen, scores, NEGATIVE)
        top = jnp.max(scores, axis=1, keepdims=True)
        weights = jnp.where(seen, jnp.exp(scores - top), 0.0)
        total = jnp.sum(weights, axis=1, keepdims=True)
        mixed = (
            jnp.dot(
                weights.astype(jnp.bfloat16), value_ref[:, cols], preferred_element_type=jnp.float32
            )
            / total
        )
        lse = top + jnp.log(total)
        for sub in range(per_kv):
            head = at * per_kv + sub
            part = slice(sub * tokens, (sub + 1) * tokens)
            tree_ref[:, head * 128 : (head + 1) * 128] = mixed[part]
            tree_lse_ref[:, head : head + 1] = lse[part]

    work = [keys_work, values_work] + [functools.partial(tree_work, at) for at in range(local_kv)]
    order = sorted(range(2, count, 2), key=lambda d: (-lowest(d), d))
    for distance in order:
        if work:
            work.pop(0)()
        hand_on(distance)
    for rest in work:
        rest()
    for distance in range(1, count, 2):
        hand_on(distance)
    for copy in wide_sent + sent:
        copy.wait_send()


def layer_front(
    hidden, in_gain, w_query, w_key, w_value, w_gate, q_gain, k_gain, cosine, sine, seen, count, kv_count, score_scale
):
    tokens = hidden.shape[0]
    width = w_query.shape[1]
    vmem = pl.BlockSpec(memory_space=pltpu.VMEM)
    hbm = pl.BlockSpec(memory_space=pltpu.HBM)
    return pl.pallas_call(
        functools.partial(layer_kernel, count, kv_count, score_scale),
        out_shape=(
            jax.ShapeDtypeStruct((count, tokens, width), jnp.bfloat16),
            jax.ShapeDtypeStruct((tokens, w_key.shape[1]), jnp.bfloat16),
            jax.ShapeDtypeStruct((tokens, w_value.shape[1]), jnp.bfloat16),
            jax.ShapeDtypeStruct((tokens, width), jnp.float32),
            jax.ShapeDtypeStruct((tokens, 128), jnp.float32),
            jax.ShapeDtypeStruct((tokens, w_gate.shape[0]), jnp.float32),
        ),
        in_specs=[hbm] * 8 + [vmem] * 3,
        out_specs=(vmem,) * 6,
        scratch_shapes=[
            pltpu.VMEM((kv_count,) + hidden.shape, hidden.dtype),
            pltpu.VMEM(w_query.shape, w_query.dtype),
            pltpu.VMEM(w_key.shape, w_key.dtype),
            pltpu.VMEM(w_value.shape, w_value.dtype),
            pltpu.VMEM(w_gate.shape, w_gate.dtype),
            pltpu.VMEM((1, in_gain.shape[0]), jnp.float32),
            pltpu.VMEM((1, 128), jnp.float32),
            pltpu.VMEM((1, 128), jnp.float32),
            pltpu.SemaphoreType.DMA((8,)),
            pltpu.SemaphoreType.DMA((kv_count,)),
            pltpu.SemaphoreType.DMA((kv_count,)),
            pltpu.SemaphoreType.DMA((count,)),
            pltpu.SemaphoreType.DMA((count,)),
        ],
        compiler_params=pltpu.CompilerParams(
            collective_id=0, has_side_effects=True, vmem_limit_bytes=60 * 2**20
        ),
        name="layer_front",
    )(hidden, in_gain[None], w_query, w_key, w_value, w_gate, q_gain[None], k_gain[None], cosine, sine, seen)


def merge_kernel(
    count,
    kv_count,
    part_ref,
    lse_ref,
    tree_ref,
    tree_lse_ref,
    gate_ref,
    w_out_ref,
    hidden_ref,
    out_ref,
    got,
    got_lse,
    mine_lse,
    held,
    held_lse,
    w_out,
    attended,
    outgoing,
    arrived,
    send_sem,
    recv_sem,
    load_sem,
    out_send,
    out_recv,
):
    me = lax.axis_index("seq")
    kv = lax.axis_index("kv")
    heads = part_ref.shape[2] // 128
    load = pltpu.make_async_copy(w_out_ref, w_out, load_sem)
    load.start()
    rows = part_ref.shape[1]

    def across(level):
        turned = jnp.transpose(level)[:8]
        return jnp.concatenate([turned] * (128 // rows), axis=1)

    for distance in range(count):
        mine_lse[distance] = across(lse_ref[flip(me, distance)])
    greet(me, count, kv, kv_count)

    def messages(distance):
        owner = flip(me, distance)
        if distance % 2:
            sources = (part_ref.at[owner], mine_lse.at[distance])
        else:
            sources = (held.at[distance // 2], held_lse.at[distance // 2])
        return [
            pltpu.make_async_remote_copy(
                src_ref=source,
                dst_ref=target.at[distance],
                send_sem=send_sem.at[which, distance],
                recv_sem=recv_sem.at[which, distance],
                device_id={"seq": flip(me, lowest(distance))},
            )
            for which, (source, target) in enumerate(zip(sources, (got, got_lse)))
        ]

    sent = []

    def send(distance):
        for copy in messages(distance):
            copy.start()
            sent.append(copy)

    for distance in sorted(range(1, count, 2), reverse=True):
        send(distance)
    evens = sorted(range(2, count, 2), key=lambda d: (lowest(d), -d))
    for distance in evens + [0]:
        owner = flip(me, distance)
        incoming = [distance | bit for bit in one_bits(lowest(distance) if distance else count)]
        for message in incoming:
            for copy in messages(message):
                copy.wait_recv()
        levels = [mine_lse[distance]] + [got_lse[message] for message in incoming]
        if not distance:
            levels.append(across(tree_lse_ref[...]))
        top = functools.reduce(jnp.maximum, levels)
        shares = [jnp.exp(level - top) for level in levels]
        total = functools.reduce(jnp.add, shares)
        inverse = 1.0 / total
        shares = [jnp.transpose(share * inverse)[:rows] for share in shares]
        if distance:
            held_lse[distance // 2] = top + jnp.log(total)
        for head in range(heads):
            cols = slice(head * 128, (head + 1) * 128)
            pieces = [part_ref[owner, :, cols]] + [got[message, :, cols] for message in incoming]
            if not distance:
                pieces.append(tree_ref[:, cols])
            mixed = functools.reduce(
                jnp.add,
                [
                    piece.astype(jnp.float32) * share[:, head : head + 1]
                    for piece, share in zip(pieces, shares)
                ],
            )
            if distance:
                held[distance // 2, :, cols] = mixed.astype(held.dtype)
            else:
                attended[:, cols] = (mixed * gate_ref[:, head : head + 1]).astype(jnp.bfloat16)
        if distance:
            send(distance)
    load.wait()
    width = out_ref.shape[1]

    def projected(target):
        cols = pl.ds(pl.multiple_of(target * width, 128), width)
        return jnp.dot(attended[...], w_out[:, cols], preferred_element_type=jnp.float32)

    def out_message(hop):
        return pltpu.make_async_remote_copy(
            src_ref=outgoing.at[hop],
            dst_ref=arrived.at[hop],
            send_sem=out_send.at[hop],
            recv_sem=out_recv.at[hop],
            device_id={"kv": (kv + hop) % kv_count},
        )

    for hop in range(1, kv_count):
        outgoing[hop] = projected((kv + hop) % kv_count).astype(jnp.bfloat16)
        copy = out_message(hop)
        copy.start()
        sent.append(copy)
    total = projected(kv)
    for hop in range(1, kv_count):
        out_message(hop).wait_recv()
        total = total + arrived[hop].astype(jnp.float32)
    out_ref[...] = (total + hidden_ref[...].astype(jnp.float32)).astype(jnp.bfloat16)
    for copy in sent:
        copy.wait_send()


def merge_parts(parts, lse, tree_mix, tree_lse, gate, w_out, hidden, count, kv_count):
    rows, width = parts.shape[1:]
    lanes = lse.shape[2]
    half = max(1, count // 2)
    vmem = pl.BlockSpec(memory_space=pltpu.VMEM)
    return pl.pallas_call(
        functools.partial(merge_kernel, count, kv_count),
        out_shape=jax.ShapeDtypeStruct(hidden.shape, jnp.bfloat16),
        in_specs=[vmem] * 5 + [pl.BlockSpec(memory_space=pltpu.HBM), vmem],
        out_specs=vmem,
        scratch_shapes=[
            pltpu.VMEM((count, rows, width), parts.dtype),
            pltpu.VMEM((count, 8, lanes), jnp.float32),
            pltpu.VMEM((count, 8, lanes), jnp.float32),
            pltpu.VMEM((half, rows, width), parts.dtype),
            pltpu.VMEM((half, 8, lanes), jnp.float32),
            pltpu.VMEM(w_out.shape, w_out.dtype),
            pltpu.VMEM((rows, width), jnp.bfloat16),
            pltpu.VMEM((kv_count,) + hidden.shape, jnp.bfloat16),
            pltpu.VMEM((kv_count,) + hidden.shape, jnp.bfloat16),
            pltpu.SemaphoreType.DMA((2, count)),
            pltpu.SemaphoreType.DMA((2, count)),
            pltpu.SemaphoreType.DMA,
            pltpu.SemaphoreType.DMA((kv_count,)),
            pltpu.SemaphoreType.DMA((kv_count,)),
        ],
        compiler_params=pltpu.CompilerParams(
            collective_id=1, has_side_effects=True, vmem_limit_bytes=60 * 2**20
        ),
        name="merge_parts",
    )(parts, lse, tree_mix, tree_lse, gate, w_out, hidden)


def pool_kernel(
    groups,
    per_kv,
    block,
    score_scale,
    facts_ref,
    q_ref,
    k_ref,
    v_ref,
    o_ref,
    lse_ref,
    first_ref,
    last_ref,
    member_ref,
    filled_ref,
):
    requests, tree, width = q_ref.shape
    local_kv = k_ref.shape[1] // 128
    per_group = requests // groups
    base_two = score_scale / math.log(2.0)
    pool_dev = k_ref.shape[0]
    offset = lax.axis_index("seq") * pool_dev

    def place(segment, start, length):
        stop = start + length
        first_ref[segment] = jnp.clip(start - offset, 0, pool_dev)
        last_ref[segment] = jnp.clip(stop - offset, 0, pool_dev)
        return stop

    def place_prefix(group, start):
        filled_ref[group] = 0
        return place(group, start, facts_ref[group])

    def place_own(owner, start):
        group = facts_ref[groups + requests + owner]
        at = filled_ref[group]
        member_ref[group * per_group + at] = owner
        filled_ref[group] = at + 1
        return place(groups + owner, start, facts_ref[groups + owner])

    lax.fori_loop(0, requests, place_own, lax.fori_loop(0, groups, place_prefix, 0))
    o_ref[...] = jnp.zeros_like(o_ref)
    lse_ref[...] = jnp.full(lse_ref.shape, NEGATIVE, jnp.float32)

    def attend(owners, first, last):
        count = len(owners) * per_kv * tree
        together = min(local_kv, 2 if len(owners) > 1 else 4)
        for base in range(0, local_kv, together):
            heads = range(base, base + together)
            rows = [
                [(owner, kv * per_kv + sub) for sub in range(per_kv) for owner in owners]
                for kv in heads
            ]
            queries = [
                jnp.concatenate(
                    [q_ref[owner, :, head * 128 : (head + 1) * 128] for owner, head in places], axis=0
                )
                for places in rows
            ]

            def visit(step, carry):
                start = pl.multiple_of(step * block, block)
                slots = start + lax.broadcasted_iota(jnp.int32, (1, block), 1)
                shown = (slots >= first) & (slots < last)
                out = []
                raw = [
                    lax.dot_general(
                        query,
                        k_ref[pl.ds(start, block), kv * 128 : (kv + 1) * 128],
                        (((1,), (1,)), ((), ())),
                        preferred_element_type=jnp.float32,
                    )
                    for kv, query in zip(heads, queries)
                ]
                for kv, scores, (run_max, run_sum, run_num) in zip(heads, raw, carry):
                    scores = jnp.where(shown, scores, NEGATIVE)
                    new_max = jnp.maximum(run_max, jnp.max(scores, axis=1, keepdims=True))
                    weights = jnp.exp2((scores - new_max) * base_two)
                    factor = jnp.exp2((run_max - new_max) * base_two)
                    run_sum = run_sum * factor + jnp.sum(weights, axis=1, keepdims=True)
                    run_num = run_num * factor + jnp.dot(
                        weights.astype(jnp.bfloat16),
                        v_ref[pl.ds(start, block), kv * 128 : (kv + 1) * 128],
                        preferred_element_type=jnp.float32,
                    )
                    out.append((new_max, run_sum, run_num))
                return tuple(out)

            empty = (
                jnp.full((count, 1), NEGATIVE, jnp.float32),
                jnp.zeros((count, 1), jnp.float32),
                jnp.zeros((count, 128), jnp.float32),
            )
            done = lax.fori_loop(
                first // block, (last + block - 1) // block, visit, (empty,) * together
            )
            for places, (run_max, run_sum, run_num) in zip(rows, done):
                mixed = (run_num / run_sum).astype(o_ref.dtype)
                lse = run_max * score_scale + jnp.log(run_sum)
                for place, (owner, head) in enumerate(places):
                    part = slice(place * tree, (place + 1) * tree)
                    o_ref[owner, :, head * 128 : (head + 1) * 128] = mixed[part]
                    lse_ref[owner, :, head : head + 1] = lse[part]

    def group_step(group, unused):
        first, last = first_ref[group], last_ref[group]

        @pl.when(last > first)
        def _():
            attend([member_ref[group * per_group + at] for at in range(per_group)], first, last)

        return unused

    def own_step(owner, unused):
        first, last = first_ref[groups + owner], last_ref[groups + owner]

        @pl.when(last > first)
        def _():
            attend([owner], first, last)

        return unused

    lax.fori_loop(0, groups, group_step, 0)
    lax.fori_loop(0, requests, own_step, 0)


def pool_attention(facts, query, keys, values, groups, per_kv, score_scale):
    requests, tree, width = query.shape
    vmem = pl.BlockSpec(memory_space=pltpu.VMEM)
    smem = pl.BlockSpec(memory_space=pltpu.SMEM)
    return pl.pallas_call(
        functools.partial(pool_kernel, groups, per_kv, min(512, keys.shape[0]), score_scale),
        out_shape=(
            jax.ShapeDtypeStruct(query.shape, jnp.bfloat16),
            jax.ShapeDtypeStruct((requests, tree, 128), jnp.float32),
        ),
        in_specs=[smem, vmem, vmem, vmem],
        out_specs=(vmem, vmem),
        scratch_shapes=[
            pltpu.SMEM((groups + requests,), jnp.int32),
            pltpu.SMEM((groups + requests,), jnp.int32),
            pltpu.SMEM((requests,), jnp.int32),
            pltpu.SMEM((groups,), jnp.int32),
        ],
        compiler_params=pltpu.CompilerParams(vmem_limit_bytes=48 * 2**20),
        name="pool_attention",
    )(facts, query, keys, values)


def body(
    hidden,
    in_gain,
    w_query,
    key_projection_weight,
    value_projection_weight,
    w_gate,
    w_out,
    q_gain,
    k_gain,
    cache_keys,
    pooled_cache_values,
    prefix_len,
    own_len,
    request_group,
    parents,
    accepted_leaf,
):
    local_req, tree = parents.shape
    groups = prefix_len.shape[0]
    requests = own_len.shape[0]
    head_width = q_gain.shape[0]
    local_heads = w_gate.shape[1]
    local_kv = key_projection_weight.shape[1] // head_width
    per_kv = local_heads // local_kv
    local_tok = hidden.shape[0]
    pool_dev = cache_keys.shape[0]
    seq_index = lax.axis_index("seq")
    score_scale = 1.0 / math.sqrt(head_width)
    seq_count = requests // local_req
    kv_count = in_gain.shape[0] // hidden.shape[1]
    reach, depth_f = tree_paths(parents)
    all_reqs = jnp.arange(requests, dtype=jnp.int32)
    my_reqs = seq_index * local_req + jnp.arange(local_req, dtype=jnp.int32)
    my_pick = (my_reqs[:, None] == all_reqs[None, :]).astype(jnp.int32)
    my_group = jnp.sum(my_pick * request_group[None, :], axis=1)
    group_ids = jnp.arange(groups, dtype=jnp.int32)
    group_pick = (my_group[:, None] == group_ids[None, :]).astype(jnp.int32)
    context = jnp.sum(group_pick * prefix_len[None, :], axis=1) + jnp.sum(
        my_pick * own_len[None, :], axis=1
    )
    positions = (context[:, None].astype(jnp.float32) + depth_f).reshape(-1)
    cosine, sine = rope_tables(positions, head_width)
    seen = (reach[:, :, None, :] * jnp.eye(local_req, dtype=jnp.float32)[:, None, :, None]).reshape(
        local_tok, local_tok
    )
    gathered, key_new, value_new, tree_mix, tree_lse, gate = layer_front(
        hidden,
        in_gain,
        w_query,
        key_projection_weight,
        value_projection_weight,
        w_gate.T,
        q_gain,
        k_gain,
        cosine,
        sine,
        seen,
        seq_count,
        kv_count,
        score_scale,
    )
    parts, part_lse = pool_attention(
        jnp.concatenate([prefix_len, own_len, request_group]),
        gathered.reshape(requests, tree, local_heads * head_width),
        cache_keys.reshape(pool_dev, local_kv * head_width),
        pooled_cache_values.reshape(pool_dev, local_kv * head_width),
        groups,
        per_kv,
        score_scale,
    )
    layer_out = merge_parts(
        parts.reshape(seq_count, local_tok, local_heads * head_width),
        part_lse.reshape(seq_count, local_tok, 128),
        tree_mix,
        tree_lse,
        gate,
        w_out,
        hidden,
        seq_count,
        kv_count,
    )
    tree_rows = jnp.concatenate(
        [
            key_new.reshape(local_req, tree, local_kv * head_width),
            value_new.reshape(local_req, tree, local_kv * head_width),
        ],
        axis=-1,
    )
    picked = accepted_rows(reach, depth_f, accepted_leaf, tree_rows)
    accepted_keys = picked[:, :, : local_kv * head_width]
    accepted_values = picked[:, :, local_kv * head_width :]
    return (layer_out, accepted_keys, accepted_values)


def solution(mesh):
    in_specs = (
        P("seq", "kv"),
        P(),
        P(None, "kv"),
        P(None, "kv"),
        P(None, "kv"),
        P(None, "kv"),
        P("kv", None),
        P(),
        P(),
        P("seq", "kv", None),
        P("seq", "kv", None),
        P(),
        P(),
        P(),
        P("seq", None),
        P("seq"),
    )
    out_specs = (P("seq", "kv"), P("seq", None, "kv"), P("seq", None, "kv"))
    return jax.shard_map(body, mesh=mesh, in_specs=in_specs, out_specs=out_specs, check_vma=False)
```
